256 devices in a mesh: section: 8 (over z_hi, y), dp: 4 (over x), expert: 8 (over z_lo, core).
Axes of the slice: x: 4, y: 4, z: 8 (z_hi: 2, z_lo: 4; z = z_hi * 4 + z_lo), core: 2. Of those that a mesh axis runs over, the one named last changes fastest.
Arguments:
- tokens: bfloat16 [4, 1024, 2048], P(None, ('dp', 'expert')), may hold values from -6 to 6
- cotangent: bfloat16 [4, 1024, 2048], P(None, ('dp', 'expert')), may hold values from -0.29882812 to 0.29882812
- up_proj: bfloat16 [8, 8, 2048, 512], P('section', 'expert'), may hold values from -0.125 to 0.125
- down_proj: bfloat16 [8, 8, 512, 2048], P('section', 'expert'), may hold values from -0.25 to 0.25
- gate_proj: bfloat16 [8, 2048, 8], P('section'), may hold values from -0.125 to 0.125
- routes: int32 [8, 4, 1024, 4], P('section', None, ('dp', 'expert')), may hold values from 0 to 7, all different within a row; in each aligned block of 32 rows (0 to 31, 32 to 63, ..., all dimensions but the last counted through in order) at most 17 rows name the same one
Outputs:
- up_grad: bfloat16 [8, 8, 2048, 512], P('section', 'expert')
- down_grad: bfloat16 [8, 8, 512, 2048], P('section', 'expert')
The draws below stay inside these ranges and needn't reach their ends.
Inputs may be any that keep to these rules, and one draw needn't show every extreme that they name: `routes`: each row names 4 different experts. Within one layer and micro-batch, the 32 rows of one device name any one expert at most 17 times, a bound that some block reaches.
All inputs are finite; a program needn't handle non-finite values.
Results may differ from the reference program's by a relative error of at most 0.025.
Values may be sent and summed in bfloat16 or wider, within the bound.
A program may use at most 128 MiB of HBM per device.

```python
import math
import jax
import jax.numpy as jnp
import numpy as np
from jax import lax

D = 2048
H = 512
EXPERTS = 8
TOPK = 4
MICRO = 4
TOK_DEV = 32
SECTIONS = 8
ROWS = 1024
CAP = 17


def level_of(key, shape, pieces, low, top_value):
    factor_of = 1.0
    for position, blocks in pieces:
        heights = jax.random.uniform(jax.random.fold_in(jax.random.fold_in(key, 6), position), (blocks,), jnp.float32, low / len(pieces), top_value / len(pieces))
        factor_of = factor_of * jnp.repeat(jnp.exp(heights), shape[position] // blocks).reshape((-1,) + (1,) * (len(shape) - 1 - position))
    return factor_of


def routed_block(stream_key, own, number, rows, number_of, top, most, slope):
    ranking = jax.random.permutation(stream_key, number_of)
    packed, common = shares(number_of, rows * top, most, slope, True), shares(number_of, rows * top, most, slope, False)
    places = jnp.arange(number_of)

    def named(sizes, offset_by):
        used = int((sizes > 0).sum())
        fixed = max(1, used // 4)
        moved = fixed + (places - fixed + offset_by * (used - fixed)) % max(1, number_of - fixed)
        return jnp.zeros((number_of,), jnp.int32).at[ranking[jnp.where(places < fixed, places, moved)]].set(jnp.asarray(sizes, jnp.int32))

    sizes = jnp.where(number % 4 == 0, named(packed, number // 4), named(common, number - number // 4 - 1))
    mixed = jax.random.permutation(jax.random.fold_in(own, 3), number_of)
    giver, sink = mixed[0:number_of // 2 * 2:2], mixed[1:number_of // 2 * 2:2]
    slack = jnp.minimum(sizes[giver] - 1, most - sizes[sink]) // 2
    slack = jnp.where((giver == ranking[0]) | (sink == ranking[0]) | (sizes[sink] == 0), 0, jnp.maximum(slack, 0))
    moved = jax.random.randint(jax.random.fold_in(own, 4), (number_of // 2,), 0, 1 << 20) % (slack + 1)
    sizes = sizes.at[giver].add(-moved).at[sink].add(moved)
    members = jnp.searchsorted(jnp.cumsum(sizes), jnp.arange(rows * top), side="right").astype(jnp.int32)
    grid = members.reshape(top, rows).T
    grid = grid[jax.random.permutation(jax.random.fold_in(own, 1), rows)]
    offset_by = jax.random.randint(jax.random.fold_in(own, 2), (rows, 1), 0, top)
    return jnp.take_along_axis(grid, (jnp.arange(top)[None, :] + offset_by) % top, axis=1)


def shares(amount, total, bound, skew, full):
    portions = [(1 << 20) // math.isqrt(grade ** skew) + 1 for grade in range(1, amount + 1)]
    largest = bound if full else min(bound, max(-(-total // amount), total * portions[0] // sum(portions)))
    least = 1 if total - largest >= amount - 1 else 0
    given, rest = [largest] + [least] * (amount - 1), total - largest - least * (amount - 1)
    while rest > 0:
        movable = [i for i in range(1, amount) if given[i] < largest] or [i for i in range(1, amount) if given[i] < bound]
        whole, remaining = sum([portions[i] for i in movable]), rest
        for i in movable:
            more = min(bound - given[i], max(1, remaining * portions[i] // whole), rest)
            given[i] = given[i] + more
            rest = rest - more
    return np.array(given)


def noise(key, dims, spread, reach, cuts=(), kind=jnp.bfloat16):
    result = spread * jax.random.normal(key, dims, jnp.float32)
    if cuts:
        result = result * level_of(key, dims, cuts, -0.22, 0.18)
    return jnp.clip(result, -reach, reach).astype(kind)


def setup_inputs(seed: int = 0) -> dict:
    streams_of = jax.random.split(jax.random.key(seed), 7)
    tokens = noise(streams_of[0], (MICRO, ROWS, D), 1.0, 6.0, ((1, 32),))
    cotangent = noise(streams_of[1], (MICRO, ROWS, D), 0.05, 0.29882812, ((1, 32),))
    up_proj = noise(streams_of[2], (SECTIONS, EXPERTS, D, H), D ** -0.5, 0.125, ((0, 8), (1, 8)))
    down_proj = noise(streams_of[3], (SECTIONS, EXPERTS, H, D), H ** -0.5, 0.25, ((0, 8), (1, 8)))
    gate_proj = noise(streams_of[4], (SECTIONS, D, EXPERTS), D ** -0.5, 0.125, ((0, 8),))
    routes_keys = jax.random.split(jax.random.fold_in(streams_of[5], 1), SECTIONS * MICRO * ROWS // TOK_DEV)
    routes_turns = jax.random.permutation(jax.random.fold_in(streams_of[5], 3), SECTIONS * MICRO * ROWS // TOK_DEV)
    routes = jax.vmap(lambda own, number: routed_block(jax.random.fold_in(streams_of[5], 2), own, number, TOK_DEV, EXPERTS, TOPK, CAP, 1))(routes_keys, routes_turns).reshape((SECTIONS, MICRO, ROWS, TOPK))
    return dict(tokens=tokens, cotangent=cotangent, up_proj=up_proj, down_proj=down_proj, gate_proj=gate_proj, routes=routes)


epsilon = 1e-06

def rounded(values):
    return lax.optimization_barrier(values.astype(jnp.bfloat16))

def normalize(section_in):
    as_f32 = section_in.astype(jnp.float32)
    rscale = lax.rsqrt(lax.optimization_barrier(jnp.mean(as_f32 * as_f32, axis=-1, keepdims=True)) + epsilon)
    return (as_f32, rscale, rounded(as_f32 * rscale))

def slot_places(route_ids):
    blocks = ROWS // TOK_DEV
    flat_ids = route_ids.reshape(MICRO, blocks, TOK_DEV * TOPK)
    onehot = (flat_ids[..., None] == jnp.arange(EXPERTS, dtype=jnp.int32)).astype(jnp.int32)
    ranks = jnp.cumsum(onehot, axis=2) - onehot
    slots = lax.optimization_barrier(jnp.sum(ranks * onehot, axis=-1)).astype(jnp.int32)
    return (flat_ids * CAP + slots).astype(jnp.int32)

def place_rows(row_values, places):

    def fill_one(values, where_to):
        return jnp.zeros((EXPERTS * CAP, values.shape[-1]), values.dtype).at[where_to].set(values)
    return jax.vmap(jax.vmap(fill_one))(row_values, places)

def pick_rows(buffer, places):

    def take_one(rows_in, where_from):
        return rows_in[where_from]
    return jax.vmap(jax.vmap(take_one))(buffer, places)

def layer_forward(section_in, route_ids, up_layer, down_layer, gate_layer):
    blocks = ROWS // TOK_DEV
    as_f32, rscale, normed = normalize(section_in)
    logits = jnp.dot(normed.reshape(-1, D), gate_layer, preferred_element_type=jnp.float32).reshape(MICRO, ROWS, EXPERTS)
    gatev = jax.nn.sigmoid(jnp.take_along_axis(logits, route_ids, axis=2))
    wgt = gatev / lax.optimization_barrier(jnp.sum(gatev, axis=-1, keepdims=True))
    places = slot_places(route_ids)
    repeated = jnp.broadcast_to(normed[:, :, None, :], (MICRO, ROWS, TOPK, D)).reshape(MICRO, blocks, TOK_DEV * TOPK, D)
    inbuf = place_rows(repeated, places).reshape(MICRO, blocks, EXPERTS, CAP, D)
    preact = jnp.einsum('mbecd,edh->mbech', inbuf.astype(jnp.float32), up_layer.astype(jnp.float32))
    hidden = rounded(jax.nn.gelu(preact))
    outbuf = rounded(jnp.einsum('mbech,ehd->mbecd', hidden.astype(jnp.float32), down_layer.astype(jnp.float32)))
    expout = pick_rows(outbuf.reshape(MICRO, blocks, EXPERTS * CAP, D), places).reshape(MICRO, ROWS, TOPK, D)
    section_out = (as_f32 + lax.optimization_barrier(jnp.sum(wgt[..., None] * expout.astype(jnp.float32), axis=2))).astype(jnp.bfloat16)
    saved = (as_f32, rscale, gatev, wgt, places, inbuf, preact, hidden, expout)
    return (section_out, saved)

def layer_backward(grad_out, section_in, route_ids, up_layer, down_layer, gate_layer):
    blocks = ROWS // TOK_DEV
    _, saved = layer_forward(section_in, route_ids, up_layer, down_layer, gate_layer)
    as_f32, rscale, gatev, wgt, places, inbuf, preact, hidden, expout = saved
    grad_f32 = grad_out.astype(jnp.float32)
    dwgt = lax.optimization_barrier(jnp.sum(expout.astype(jnp.float32) * grad_f32[:, :, None, :], axis=-1))
    dout = rounded(wgt[..., None] * grad_f32[:, :, None, :]).reshape(MICRO, blocks, TOK_DEV * TOPK, D)
    dbuf = place_rows(dout, places).reshape(MICRO, blocks, EXPERTS, CAP, D)
    down_part = jnp.einsum('mbech,mbecd->ehd', hidden.astype(jnp.float32), dbuf.astype(jnp.float32))
    dhidden = jnp.einsum('mbecd,ehd->mbech', dbuf.astype(jnp.float32), down_layer.astype(jnp.float32))
    _, pullback = jax.vjp(jax.nn.gelu, preact)
    dpre = rounded(pullback(dhidden)[0])
    up_part = jnp.einsum('mbecd,mbech->edh', inbuf.astype(jnp.float32), dpre.astype(jnp.float32))
    dinbuf = rounded(jnp.einsum('mbech,edh->mbecd', dpre.astype(jnp.float32), up_layer.astype(jnp.float32)))
    dexp = lax.optimization_barrier(jnp.sum(pick_rows(dinbuf.reshape(MICRO, blocks, EXPERTS * CAP, D), places).reshape(MICRO, ROWS, TOPK, D).astype(jnp.float32), axis=2))
    total = lax.optimization_barrier(jnp.sum(gatev, axis=-1, keepdims=True))
    dgate = (dwgt - lax.optimization_barrier(jnp.sum(wgt * dwgt, axis=-1, keepdims=True))) / total
    dlogit = dgate * gatev * (1.0 - gatev)
    onehot = (route_ids[..., None] == jnp.arange(EXPERTS, dtype=jnp.int32)).astype(jnp.float32)
    dfull = lax.optimization_barrier(jnp.sum(dlogit[..., None] * onehot, axis=2))
    drouter = jnp.dot(dfull.reshape(-1, EXPERTS), gate_layer.astype(jnp.float32).T, precision=lax.Precision.HIGHEST).reshape(MICRO, ROWS, D)
    dnorm = dexp + drouter
    grad_in = rounded(grad_f32 + rscale * dnorm - as_f32 * rscale ** 3 * lax.optimization_barrier(jnp.mean(dnorm * as_f32, axis=-1, keepdims=True)))
    return (grad_in, up_part, down_part)

def reference(tokens, cotangent, up_proj, down_proj, gate_proj, routes):
    inputs_kept = []
    current = tokens
    for layer in range(SECTIONS):
        inputs_kept.append(current)
        current, _ = layer_forward(current, routes[layer], up_proj[layer], down_proj[layer], gate_proj[layer])
    grad_now = cotangent
    up_parts = [None] * SECTIONS
    down_parts = [None] * SECTIONS
    for layer in reversed(range(SECTIONS)):
        grad_now, up_part, down_part = layer_backward(grad_now, inputs_kept[layer], routes[layer], up_proj[layer], down_proj[layer], gate_proj[layer])
        up_parts[layer] = up_part
        down_parts[layer] = down_part
    return (jnp.stack(up_parts).astype(jnp.bfloat16), jnp.stack(down_parts).astype(jnp.bfloat16))
```

```python
import functools

import jax
import jax.numpy as jnp
from jax import lax
from jax.experimental import pallas as pl
from jax.experimental.pallas import tpu as pltpu
from jax.sharding import PartitionSpec as P

MESH = pl.DeviceIdType.MESH

CAP = 17


epsilon = 1e-06


def from_behind(block, axis, distance):
    devices = range(lax.axis_size(axis))
    route = [(i - distance, i) for i in devices if i - distance in devices]
    return lax.ppermute(block, axis, route)


def exchange_kernel(n, x_ref, o_ref, copy_sem, send_sem, recv_sem):
    me = lax.axis_index("expert")
    barrier = pltpu.get_barrier_semaphore()
    for j in range(1, n):
        pl.semaphore_signal(
            barrier, inc=1, device_id={"expert": lax.rem(me + j, n)}, device_id_type=MESH
        )
    pl.semaphore_wait(barrier, n - 1)
    local = pltpu.make_async_copy(x_ref.at[me], o_ref.at[me], copy_sem)
    local.start()
    copies = []
    for j in range(1, n):
        peer = lax.rem(me + j, n)
        copy = pltpu.make_async_remote_copy(
            src_ref=x_ref.at[peer],
            dst_ref=o_ref.at[me],
            send_sem=send_sem.at[j],
            recv_sem=recv_sem.at[j],
            device_id={"expert": peer},
            device_id_type=MESH,
        )
        copy.start()
        copies.append(copy)
    local.wait()
    for copy in copies:
        copy.wait()


def expert_exchange(block, site):
    n = block.shape[0]
    nbytes = block.size * block.dtype.itemsize
    return pl.pallas_call(
        functools.partial(exchange_kernel, n),
        out_shape=jax.ShapeDtypeStruct(block.shape, block.dtype),
        in_specs=[pl.BlockSpec(memory_space=pl.ANY)],
        out_specs=pl.BlockSpec(memory_space=pl.ANY),
        scratch_shapes=[
            pltpu.SemaphoreType.DMA(()),
            pltpu.SemaphoreType.DMA((n,)),
            pltpu.SemaphoreType.DMA((n,)),
        ],
        compiler_params=pltpu.CompilerParams(collective_id=site, has_side_effects=True),
        cost_estimate=pl.CostEstimate(flops=0, bytes_accessed=2 * nbytes, transcendentals=0),
    )(block)


def normalize(section_in):
    as_f32 = section_in.astype(jnp.float32)
    rscale = lax.rsqrt(jnp.mean(as_f32 * as_f32, axis=-1, keepdims=True) + epsilon)
    return (as_f32, rscale, (as_f32 * rscale).astype(jnp.bfloat16))


def local(tokens, cotangent, up_proj, down_proj, gate_proj, routes):
    section_pos = lax.axis_index("section")
    section_count = lax.axis_size("section")
    expert_devs = lax.axis_size("expert")
    local_experts = up_proj.shape[1]
    experts_all = local_experts * expert_devs
    micro_count, tok_rows, features = tokens.shape
    top_count = routes.shape[3]
    capacity = CAP
    w_up = up_proj[0]
    w_down = down_proj[0]
    gate_cols = gate_proj[0]
    route_all = routes[0]
    step_count = micro_count + section_count - 1
    expert_ids = jnp.arange(experts_all, dtype=jnp.int32)

    def slot_rows(route_rows):
        flat_ids = route_rows.reshape(-1)
        onehot = (flat_ids[:, None] == expert_ids[None, :]).astype(jnp.int32)
        ranks = jnp.cumsum(onehot, axis=0) - onehot
        slots = jnp.sum(ranks * onehot, axis=1)
        return flat_ids * capacity + slots

    def to_buffer(row_values, dest_rows):
        filled = (
            jnp.zeros((experts_all * capacity, features), row_values.dtype)
            .at[dest_rows]
            .set(row_values)
        )
        return filled.reshape(expert_devs, local_experts, capacity, features)

    def from_buffer(buffer, dest_rows):
        return buffer.reshape(experts_all * capacity, features)[dest_rows].reshape(
            tok_rows, top_count, features
        )

    def repeated(normed):
        return jnp.broadcast_to(normed[:, None, :], (tok_rows, top_count, features)).reshape(
            tok_rows * top_count, features
        )

    def gate_values(normed, route_rows):
        logits = jnp.dot(normed, gate_cols, preferred_element_type=jnp.float32)
        return jax.nn.sigmoid(jnp.take_along_axis(logits, route_rows, axis=1))

    def expert_forward(received):
        preact = jnp.einsum("secd,edh->sech", received, w_up, preferred_element_type=jnp.float32)
        hidden = jax.nn.gelu(preact).astype(jnp.bfloat16)
        outbuf = jnp.einsum(
            "sech,ehd->secd", hidden, w_down, preferred_element_type=jnp.float32
        ).astype(jnp.bfloat16)
        return (preact, outbuf)

    def expert_skip(received):
        preact = jnp.zeros(received.shape[:3] + (w_up.shape[2],), jnp.float32)
        return (preact, jnp.zeros_like(received))

    def forward_step(incoming, step_index):
        micro_raw = step_index - section_pos
        live_step = (micro_raw >= 0) & (micro_raw < micro_count)
        micro = jnp.clip(micro_raw, 0, micro_count - 1)
        first_in = lax.dynamic_index_in_dim(tokens, micro, 0, keepdims=False)
        section_in = jnp.where(section_pos == 0, first_in, incoming)
        route_rows = lax.dynamic_index_in_dim(route_all, micro, 0, keepdims=False)
        as_f32, rscale, normed = normalize(section_in)
        gatev = gate_values(normed, route_rows)
        wgt = gatev / jnp.sum(gatev, axis=-1, keepdims=True)
        dest_rows = slot_rows(route_rows)
        received = expert_exchange(to_buffer(repeated(normed), dest_rows), 3)
        preact, outbuf = lax.cond(live_step, expert_forward, expert_skip, received)
        returned = expert_exchange(outbuf, 0)
        expout = from_buffer(returned, dest_rows)
        section_out = (
            as_f32 + jnp.sum(wgt[..., None] * expout.astype(jnp.float32), axis=1)
        ).astype(jnp.bfloat16)
        passed = from_behind(section_out, "section", 1)
        stored = (section_in, gatev, expout, received, preact)
        return (passed, stored)

    start_act = jnp.zeros((tok_rows, features), jnp.bfloat16)
    _, saved = lax.scan(forward_step, start_act, jnp.arange(step_count))

    def expert_backward(received, dreceived, preact):
        hidden = jax.nn.gelu(preact).astype(jnp.bfloat16)
        down_inc = jnp.einsum(
            "sech,secd->ehd", hidden, dreceived, preferred_element_type=jnp.float32
        )
        dhidden = jnp.einsum(
            "secd,ehd->sech", dreceived, w_down, preferred_element_type=jnp.float32
        )
        _, pullback = jax.vjp(jax.nn.gelu, preact)
        dpre = pullback(dhidden)[0].astype(jnp.bfloat16)
        up_inc = jnp.einsum("secd,sech->edh", received, dpre, preferred_element_type=jnp.float32)
        dinbuf = jnp.einsum(
            "sech,edh->secd", dpre, w_up, preferred_element_type=jnp.float32
        ).astype(jnp.bfloat16)
        return (up_inc, down_inc, dinbuf)

    def backward_skip(operands):
        received = operands[0]
        return (
            jnp.zeros(w_up.shape, jnp.float32),
            jnp.zeros(w_down.shape, jnp.float32),
            jnp.zeros_like(received),
        )

    def backward_step(carry, step_index):
        incoming, acc_up, acc_down = carry
        micro_raw = step_index - (section_count - 1 - section_pos)
        live_step = (micro_raw >= 0) & (micro_raw < micro_count)
        micro = jnp.clip(micro_raw, 0, micro_count - 1)
        fwd_index = micro + section_pos
        section_in = lax.dynamic_index_in_dim(saved[0], fwd_index, 0, keepdims=False)
        gatev = lax.dynamic_index_in_dim(saved[1], fwd_index, 0, keepdims=False)
        expout = lax.dynamic_index_in_dim(saved[2], fwd_index, 0, keepdims=False)
        last_in = lax.dynamic_index_in_dim(cotangent, micro, 0, keepdims=False)
        grad_out = jnp.where(section_pos == section_count - 1, last_in, incoming)
        route_rows = lax.dynamic_index_in_dim(route_all, micro, 0, keepdims=False)
        dest_rows = slot_rows(route_rows)
        as_f32, rscale, normed = normalize(section_in)
        total = jnp.sum(gatev, axis=-1, keepdims=True)
        wgt = gatev / total
        grad_f32 = grad_out.astype(jnp.float32)
        dwgt = jnp.sum(expout.astype(jnp.float32) * grad_f32[:, None, :], axis=-1)
        dout = (
            (wgt[..., None] * grad_f32[:, None, :])
            .astype(jnp.bfloat16)
            .reshape(tok_rows * top_count, features)
        )
        dsend = to_buffer(dout, dest_rows)
        dreceived = expert_exchange(dsend, 1)
        received = lax.dynamic_index_in_dim(saved[3], fwd_index, 0, keepdims=False)
        preact = lax.dynamic_index_in_dim(saved[4], fwd_index, 0, keepdims=False)

        def backward_live(operands):
            return expert_backward(operands[0], operands[1], operands[2])

        up_inc, down_inc, dinbuf = lax.cond(
            live_step, backward_live, backward_skip, (received, dreceived, preact)
        )
        dreturned = expert_exchange(dinbuf, 2)
        dexp = jnp.sum(from_buffer(dreturned, dest_rows).astype(jnp.float32), axis=1)
        dgate = (dwgt - jnp.sum(wgt * dwgt, axis=-1, keepdims=True)) / total
        dlogit = dgate * gatev * (1.0 - gatev)
        onehot = (route_rows[..., None] == expert_ids).astype(jnp.float32)
        dfull = jnp.sum(dlogit[..., None] * onehot, axis=1)
        drouter = jnp.dot(dfull, gate_cols.astype(jnp.float32).T, precision=lax.Precision.HIGHEST)
        dnorm = dexp + drouter
        grad_in = (
            grad_f32
            + rscale * dnorm
            - as_f32 * rscale**3 * jnp.mean(dnorm * as_f32, axis=-1, keepdims=True)
        ).astype(jnp.bfloat16)
        passed = from_behind(grad_in, "section", -1)
        return ((passed, acc_up + up_inc, acc_down + down_inc), None)

    start_carry = (
        jnp.zeros((tok_rows, features), jnp.bfloat16),
        jnp.zeros(w_up.shape, jnp.float32),
        jnp.zeros(w_down.shape, jnp.float32),
    )
    final_carry, _ = lax.scan(backward_step, start_carry, jnp.arange(step_count))
    acc_up = final_carry[1]
    acc_down = final_carry[2]
    sum_up, sum_down = lax.psum((acc_up, acc_down), "dp")
    up_out = sum_up.astype(jnp.bfloat16)
    down_out = sum_down.astype(jnp.bfloat16)
    return (up_out[None], down_out[None])


def solution(mesh):
    in_specs = (
        P(None, ("dp", "expert"), None),
        P(None, ("dp", "expert"), None),
        P("section", "expert", None, None),
        P("section", "expert", None, None),
        P("section", None, None),
        P("section", None, ("dp", "expert"), None),
    )
    out_specs = (P("section", "expert", None, None), P("section", "expert", None, None))
    return jax.shard_map(local, mesh=mesh, in_specs=in_specs, out_specs=out_specs, check_vma=False)
```

```python
import functools

import jax
import jax.numpy as jnp
from jax import lax
from jax.experimental import pallas as pl
from jax.experimental.pallas import tpu as pltpu
from jax.sharding import PartitionSpec as P

MESH = pl.DeviceIdType.MESH

CAP = 17


epsilon = 1e-06


def from_behind(block, axis, distance):
    devices = range(lax.axis_size(axis))
    route = [(i - distance, i) for i in devices if i - distance in devices]
    return lax.ppermute(block, axis, route)


def exchange_kernel(n, x_ref, o_ref, copy_sem, send_sem, recv_sem):
    me = lax.axis_index("expert")
    barrier = pltpu.get_barrier_semaphore()
    for j in range(1, n):
        pl.semaphore_signal(
            barrier, inc=1, device_id={"expert": lax.rem(me + j, n)}, device_id_type=MESH
        )
    pl.semaphore_wait(barrier, n - 1)
    local = pltpu.make_async_copy(x_ref.at[me], o_ref.at[me], copy_sem)
    local.start()
    copies = []
    for j in range(1, n):
        peer = lax.rem(me + j, n)
        copy = pltpu.make_async_remote_copy(
            src_ref=x_ref.at[peer],
            dst_ref=o_ref.at[me],
            send_sem=send_sem.at[j],
            recv_sem=recv_sem.at[j],
            device_id={"expert": peer},
            device_id_type=MESH,
        )
        copy.start()
        copies.append(copy)
    local.wait()
    for copy in copies:
        copy.wait()


def expert_exchange(block, site):
    n = block.shape[0]
    nbytes = block.size * block.dtype.itemsize
    return pl.pallas_call(
        functools.partial(exchange_kernel, n),
        out_shape=jax.ShapeDtypeStruct(block.shape, block.dtype),
        in_specs=[pl.BlockSpec(memory_space=pl.ANY)],
        out_specs=pl.BlockSpec(memory_space=pl.ANY),
        scratch_shapes=[
            pltpu.SemaphoreType.DMA(()),
            pltpu.SemaphoreType.DMA((n,)),
            pltpu.SemaphoreType.DMA((n,)),
        ],
        compiler_params=pltpu.CompilerParams(collective_id=site, has_side_effects=True),
        cost_estimate=pl.CostEstimate(flops=0, bytes_accessed=2 * nbytes, transcendentals=0),
    )(block)


def normalize(section_in):
    as_f32 = section_in.astype(jnp.float32)
    rscale = lax.rsqrt(jnp.mean(as_f32 * as_f32, axis=-1, keepdims=True) + epsilon)
    return (as_f32, rscale, (as_f32 * rscale).astype(jnp.bfloat16))


def local(tokens, cotangent, up_proj, down_proj, gate_proj, routes):
    section_pos = lax.axis_index("section")
    section_count = lax.axis_size("section")
    expert_devs = lax.axis_size("expert")
    local_experts = up_proj.shape[1]
    experts_all = local_experts * expert_devs
    micro_count, tok_rows, features = tokens.shape
    top_count = routes.shape[3]
    capacity = CAP
    w_up = up_proj[0]
    w_down = down_proj[0]
    gate_cols = gate_proj[0]
    route_all = routes[0]
    step_count = micro_count + section_count - 1
    expert_ids = jnp.arange(experts_all, dtype=jnp.int32)

    def slot_rows(route_rows):
        flat_ids = route_rows.reshape(-1)
        onehot = (flat_ids[:, None] == expert_ids[None, :]).astype(jnp.int32)
        ranks = jnp.cumsum(onehot, axis=0) - onehot
        slots = jnp.sum(ranks * onehot, axis=1)
        return flat_ids * capacity + slots

    def to_buffer(row_values, dest_rows):
        filled = (
            jnp.zeros((experts_all * capacity, features), row_values.dtype)
            .at[dest_rows]
            .set(row_values)
        )
        return filled.reshape(expert_devs, local_experts, capacity, features)

    def from_buffer(buffer, dest_rows):
        return buffer.reshape(experts_all * capacity, features)[dest_rows].reshape(
            tok_rows, top_count, features
        )

    def repeated(normed):
        return jnp.broadcast_to(normed[:, None, :], (tok_rows, top_count, features)).reshape(
            tok_rows * top_count, features
        )

    def gate_values(normed, route_rows):
        logits = jnp.dot(normed, gate_cols, preferred_element_type=jnp.float32)
        return jax.nn.sigmoid(jnp.take_along_axis(logits, route_rows, axis=1))

    def expert_forward(received):
        preact = jnp.einsum("secd,edh->sech", received, w_up, preferred_element_type=jnp.float32)
        hidden = jax.nn.gelu(preact).astype(jnp.bfloat16)
        outbuf = jnp.einsum(
            "sech,ehd->secd", hidden, w_down, preferred_element_type=jnp.float32
        ).astype(jnp.bfloat16)
        return (preact, outbuf)

    def expert_skip(received):
        preact = jnp.zeros(received.shape[:3] + (w_up.shape[2],), jnp.float32)
        return (preact, jnp.zeros_like(received))

    def forward_step(incoming, step_index):
        micro_raw = step_index - section_pos
        live_step = (micro_raw >= 0) & (micro_raw < micro_count)
        micro = jnp.clip(micro_raw, 0, micro_count - 1)
        first_in = lax.dynamic_index_in_dim(tokens, micro, 0, keepdims=False)
        section_in = jnp.where(section_pos == 0, first_in, incoming)
        route_rows = lax.dynamic_index_in_dim(route_all, micro, 0, keepdims=False)
        as_f32, rscale, normed = normalize(section_in)
        gatev = gate_values(normed, route_rows)
        wgt = gatev / jnp.sum(gatev, axis=-1, keepdims=True)
        dest_rows = slot_rows(route_rows)
        received = expert_exchange(to_buffer(repeated(normed), dest_rows), 3)
        preact, outbuf = lax.cond(live_step, expert_forward, expert_skip, received)
        returned = expert_exchange(outbuf, 0)
        expout = from_buffer(returned, dest_rows)
        section_out = (
            as_f32 + jnp.sum(wgt[..., None] * expout.astype(jnp.float32), axis=1)
        ).astype(jnp.bfloat16)
        passed = from_behind(section_out, "section", 1)
        stored = (section_in, gatev, expout, received, preact)
        return (passed, stored)

    start_act = jnp.zeros((tok_rows, features), jnp.bfloat16)
    _, saved = lax.scan(forward_step, start_act, jnp.arange(step_count))

    def expert_backward(received, dreceived, preact):
        hidden = jax.nn.gelu(preact).astype(jnp.bfloat16)
        down_inc = jnp.einsum(
            "sech,secd->ehd", hidden, dreceived, preferred_element_type=jnp.float32
        )
        dhidden = jnp.einsum(
            "secd,ehd->sech", dreceived, w_down, preferred_element_type=jnp.float32
        )
        _, pullback = jax.vjp(jax.nn.gelu, preact)
        dpre = pullback(dhidden)[0].astype(jnp.bfloat16)
        up_inc = jnp.einsum("secd,sech->edh", received, dpre, preferred_element_type=jnp.float32)
        dinbuf = jnp.einsum(
            "sech,edh->secd", dpre, w_up, preferred_element_type=jnp.float32
        ).astype(jnp.bfloat16)
        return (up_inc, down_inc, dinbuf)

    def backward_skip(operands):
        received, acc_up, acc_down = operands[0], operands[3], operands[4]
        return (acc_up, acc_down, jnp.zeros_like(received))

    def backward_step(carry, step_index):
        incoming, acc_up, acc_down = carry
        micro_raw = step_index - (section_count - 1 - section_pos)
        live_step = (micro_raw >= 0) & (micro_raw < micro_count)
        micro = jnp.clip(micro_raw, 0, micro_count - 1)
        fwd_index = micro + section_pos
        section_in = lax.dynamic_index_in_dim(saved[0], fwd_index, 0, keepdims=False)
        gatev = lax.dynamic_index_in_dim(saved[1], fwd_index, 0, keepdims=False)
        expout = lax.dynamic_index_in_dim(saved[2], fwd_index, 0, keepdims=False)
        last_in = lax.dynamic_index_in_dim(cotangent, micro, 0, keepdims=False)
        grad_out = jnp.where(section_pos == section_count - 1, last_in, incoming)
        route_rows = lax.dynamic_index_in_dim(route_all, micro, 0, keepdims=False)
        dest_rows = slot_rows(route_rows)
        as_f32, rscale, normed = normalize(section_in)
        total = jnp.sum(gatev, axis=-1, keepdims=True)
        wgt = gatev / total
        grad_f32 = grad_out.astype(jnp.float32)
        dwgt = jnp.sum(expout.astype(jnp.float32) * grad_f32[:, None, :], axis=-1)
        dout = (
            (wgt[..., None] * grad_f32[:, None, :])
            .astype(jnp.bfloat16)
            .reshape(tok_rows * top_count, features)
        )
        dsend = to_buffer(dout, dest_rows)
        dreceived = expert_exchange(dsend, 1)
        received = lax.dynamic_index_in_dim(saved[3], fwd_index, 0, keepdims=False)
        preact = lax.dynamic_index_in_dim(saved[4], fwd_index, 0, keepdims=False)

        def backward_live(operands):
            up_inc, down_inc, dinbuf = expert_backward(operands[0], operands[1], operands[2])
            return (operands[3] + up_inc, operands[4] + down_inc, dinbuf)

        new_up, new_down, dinbuf = lax.cond(
            live_step,
            backward_live,
            backward_skip,
            (received, dreceived, preact, acc_up, acc_down),
        )
        dreturned = expert_exchange(dinbuf, 2)
        dexp = jnp.sum(from_buffer(dreturned, dest_rows).astype(jnp.float32), axis=1)
        dgate = (dwgt - jnp.sum(wgt * dwgt, axis=-1, keepdims=True)) / total
        dlogit = dgate * gatev * (1.0 - gatev)
        onehot = (route_rows[..., None] == expert_ids).astype(jnp.float32)
        dfull = jnp.sum(dlogit[..., None] * onehot, axis=1)
        drouter = jnp.dot(dfull, gate_cols.astype(jnp.float32).T, precision=lax.Precision.HIGHEST)
        dnorm = dexp + drouter
        grad_in = (
            grad_f32
            + rscale * dnorm
            - as_f32 * rscale**3 * jnp.mean(dnorm * as_f32, axis=-1, keepdims=True)
        ).astype(jnp.bfloat16)
        passed = from_behind(grad_in, "section", -1)
        return ((passed, new_up, new_down), None)

    start_carry = (
        jnp.zeros((tok_rows, features), jnp.bfloat16),
        jnp.zeros(w_up.shape, jnp.float32),
        jnp.zeros(w_down.shape, jnp.float32),
    )
    final_carry, _ = lax.scan(backward_step, start_carry, jnp.arange(step_count))
    acc_up = final_carry[1]
    acc_down = final_carry[2]
    sum_up, sum_down = lax.psum(
        (acc_up.astype(jnp.bfloat16), acc_down.astype(jnp.bfloat16)), "dp"
    )
    up_out = sum_up.astype(jnp.bfloat16)
    down_out = sum_down.astype(jnp.bfloat16)
    return (up_out[None], down_out[None])


def solution(mesh):
    in_specs = (
        P(None, ("dp", "expert"), None),
        P(None, ("dp", "expert"), None),
        P("section", "expert", None, None),
        P("section", "expert", None, None),
        P("section", None, None),
        P("section", None, ("dp", "expert"), None),
    )
    out_specs = (P("section", "expert", None, None), P("section", "expert", None, None))
    return jax.shard_map(local, mesh=mesh, in_specs=in_specs, out_specs=out_specs, check_vma=False)
```

```python
import functools

import jax
import jax.numpy as jnp
from jax import lax
from jax.experimental import pallas as pl
from jax.experimental.pallas import tpu as pltpu
from jax.sharding import PartitionSpec as P

MESH = pl.DeviceIdType.MESH

CAP = 17


epsilon = 1e-06


def from_behind(block, axis, distance):
    devices = range(lax.axis_size(axis))
    route = [(i - distance, i) for i in devices if i - distance in devices]
    return lax.ppermute(block, axis, route)


def exchange_kernel(n, x_ref, o_ref, copy_sem, send_sem, recv_sem):
    me = lax.axis_index("expert")
    barrier = pltpu.get_barrier_semaphore()
    for j in range(1, n):
        pl.semaphore_signal(
            barrier, inc=1, device_id={"expert": lax.rem(me + j, n)}, device_id_type=MESH
        )
    pl.semaphore_wait(barrier, n - 1)
    local = pltpu.make_async_copy(x_ref.at[me], o_ref.at[me], copy_sem)
    local.start()
    copies = []
    for j in range(1, n):
        peer = lax.rem(me + j, n)
        copy = pltpu.make_async_remote_copy(
            src_ref=x_ref.at[peer],
            dst_ref=o_ref.at[me],
            send_sem=send_sem.at[j],
            recv_sem=recv_sem.at[j],
            device_id={"expert": peer},
            device_id_type=MESH,
        )
        copy.start()
        copies.append(copy)
    local.wait()
    for copy in copies:
        copy.wait()


def expert_exchange(block, site):
    n = block.shape[0]
    nbytes = block.size * block.dtype.itemsize
    return pl.pallas_call(
        functools.partial(exchange_kernel, n),
        out_shape=jax.ShapeDtypeStruct(block.shape, block.dtype),
        in_specs=[pl.BlockSpec(memory_space=pl.ANY)],
        out_specs=pl.BlockSpec(memory_space=pl.ANY),
        scratch_shapes=[
            pltpu.SemaphoreType.DMA(()),
            pltpu.SemaphoreType.DMA((n,)),
            pltpu.SemaphoreType.DMA((n,)),
        ],
        compiler_params=pltpu.CompilerParams(collective_id=site, has_side_effects=True),
        cost_estimate=pl.CostEstimate(flops=0, bytes_accessed=2 * nbytes, transcendentals=0),
    )(block)


def normalize(section_in):
    as_f32 = section_in.astype(jnp.float32)
    rscale = lax.rsqrt(jnp.mean(as_f32 * as_f32, axis=-1, keepdims=True) + epsilon)
    return (as_f32, rscale, (as_f32 * rscale).astype(jnp.bfloat16))


def local(tokens, cotangent, up_proj, down_proj, gate_proj, routes):
    section_pos = lax.axis_index("section")
    section_count = lax.axis_size("section")
    expert_devs = lax.axis_size("expert")
    local_experts = up_proj.shape[1]
    experts_all = local_experts * expert_devs
    micro_count, tok_rows, features = tokens.shape
    top_count = routes.shape[3]
    capacity = CAP
    w_up = up_proj[0]
    w_down = down_proj[0]
    gate_cols = gate_proj[0]
    route_all = routes[0]
    step_count = micro_count + section_count - 1
    expert_ids = jnp.arange(experts_all, dtype=jnp.int32)

    def slot_rows(route_rows):
        flat_ids = route_rows.reshape(-1)
        onehot = (flat_ids[:, None] == expert_ids[None, :]).astype(jnp.int32)
        ranks = jnp.cumsum(onehot, axis=0) - onehot
        slots = jnp.sum(ranks * onehot, axis=1)
        return flat_ids * capacity + slots

    lanes = 128
    pieces = features // lanes

    def to_buffer(row_values, dest_rows):
        filled = (
            jnp.zeros((experts_all * capacity, pieces, lanes), row_values.dtype)
            .at[dest_rows]
            .set(row_values.reshape(-1, pieces, lanes))
        )
        return filled.reshape(expert_devs, local_experts * capacity * pieces, lanes)

    def from_buffer(buffer, dest_rows):
        return buffer.reshape(experts_all * capacity, pieces, lanes)[dest_rows].reshape(
            tok_rows, top_count, features
        )

    def as_rows(buffer):
        return buffer.reshape(expert_devs, local_experts, capacity, features)

    def as_pieces(buffer):
        return buffer.reshape(expert_devs, local_experts * capacity * pieces, lanes)

    def repeated(normed):
        return jnp.broadcast_to(normed[:, None, :], (tok_rows, top_count, features)).reshape(
            tok_rows * top_count, features
        )

    def gate_values(normed, route_rows):
        logits = jnp.dot(normed, gate_cols, preferred_element_type=jnp.float32)
        return jax.nn.sigmoid(jnp.take_along_axis(logits, route_rows, axis=1))

    def expert_forward(received):
        preact = jnp.einsum("secd,edh->sech", received, w_up, preferred_element_type=jnp.float32)
        hidden = jax.nn.gelu(preact).astype(jnp.bfloat16)
        outbuf = jnp.einsum(
            "sech,ehd->secd", hidden, w_down, preferred_element_type=jnp.float32
        ).astype(jnp.bfloat16)
        return (preact, outbuf)

    def expert_skip(received):
        preact = jnp.zeros(received.shape[:3] + (w_up.shape[2],), jnp.float32)
        return (preact, jnp.zeros_like(received))

    def forward_step(incoming, step_index):
        micro_raw = step_index - section_pos
        live_step = (micro_raw >= 0) & (micro_raw < micro_count)
        micro = jnp.clip(micro_raw, 0, micro_count - 1)
        first_in = lax.dynamic_index_in_dim(tokens, micro, 0, keepdims=False)
        section_in = jnp.where(section_pos == 0, first_in, incoming)
        route_rows = lax.dynamic_index_in_dim(route_all, micro, 0, keepdims=False)
        as_f32, rscale, normed = normalize(section_in)
        gatev = gate_values(normed, route_rows)
        wgt = gatev / jnp.sum(gatev, axis=-1, keepdims=True)
        dest_rows = slot_rows(route_rows)
        received = as_rows(expert_exchange(to_buffer(repeated(normed), dest_rows), 3))
        preact, outbuf = lax.cond(live_step, expert_forward, expert_skip, received)
        returned = expert_exchange(as_pieces(outbuf), 0)
        expout = from_buffer(returned, dest_rows)
        section_out = (
            as_f32 + jnp.sum(wgt[..., None] * expout.astype(jnp.float32), axis=1)
        ).astype(jnp.bfloat16)
        passed = from_behind(section_out, "section", 1)
        stored = (section_in, gatev, expout, received, preact)
        return (passed, stored)

    start_act = jnp.zeros((tok_rows, features), jnp.bfloat16)
    _, saved = lax.scan(forward_step, start_act, jnp.arange(step_count))

    def expert_backward(received, dreceived, preact):
        hidden = jax.nn.gelu(preact).astype(jnp.bfloat16)
        down_inc = jnp.einsum(
            "sech,secd->ehd", hidden, dreceived, preferred_element_type=jnp.float32
        )
        dhidden = jnp.einsum(
            "secd,ehd->sech", dreceived, w_down, preferred_element_type=jnp.float32
        )
        _, pullback = jax.vjp(jax.nn.gelu, preact)
        dpre = pullback(dhidden)[0].astype(jnp.bfloat16)
        up_inc = jnp.einsum("secd,sech->edh", received, dpre, preferred_element_type=jnp.float32)
        dinbuf = jnp.einsum(
            "sech,edh->secd", dpre, w_up, preferred_element_type=jnp.float32
        ).astype(jnp.bfloat16)
        return (up_inc, down_inc, dinbuf)

    def backward_skip(operands):
        received, acc_up, acc_down = operands[0], operands[3], operands[4]
        return (acc_up, acc_down, jnp.zeros_like(received))

    def backward_step(carry, step_index):
        incoming, acc_up, acc_down = carry
        micro_raw = step_index - (section_count - 1 - section_pos)
        live_step = (micro_raw >= 0) & (micro_raw < micro_count)
        micro = jnp.clip(micro_raw, 0, micro_count - 1)
        fwd_index = micro + section_pos
        section_in = lax.dynamic_index_in_dim(saved[0], fwd_index, 0, keepdims=False)
        gatev = lax.dynamic_index_in_dim(saved[1], fwd_index, 0, keepdims=False)
        expout = lax.dynamic_index_in_dim(saved[2], fwd_index, 0, keepdims=False)
        last_in = lax.dynamic_index_in_dim(cotangent, micro, 0, keepdims=False)
        grad_out = jnp.where(section_pos == section_count - 1, last_in, incoming)
        route_rows = lax.dynamic_index_in_dim(route_all, micro, 0, keepdims=False)
        dest_rows = slot_rows(route_rows)
        as_f32, rscale, normed = normalize(section_in)
        total = jnp.sum(gatev, axis=-1, keepdims=True)
        wgt = gatev / total
        grad_f32 = grad_out.astype(jnp.float32)
        dwgt = jnp.sum(expout.astype(jnp.float32) * grad_f32[:, None, :], axis=-1)
        dout = (
            (wgt[..., None] * grad_f32[:, None, :])
            .astype(jnp.bfloat16)
            .reshape(tok_rows * top_count, features)
        )
        dsend = to_buffer(dout, dest_rows)
        dreceived = as_rows(expert_exchange(dsend, 1))
        received = lax.dynamic_index_in_dim(saved[3], fwd_index, 0, keepdims=False)
        preact = lax.dynamic_index_in_dim(saved[4], fwd_index, 0, keepdims=False)

        def backward_live(operands):
            up_inc, down_inc, dinbuf = expert_backward(operands[0], operands[1], operands[2])
            return (operands[3] + up_inc, operands[4] + down_inc, dinbuf)

        new_up, new_down, dinbuf = lax.cond(
            live_step,
            backward_live,
            backward_skip,
            (received, dreceived, preact, acc_up, acc_down),
        )
        dreturned = expert_exchange(as_pieces(dinbuf), 2)
        dexp = jnp.sum(from_buffer(dreturned, dest_rows).astype(jnp.float32), axis=1)
        dgate = (dwgt - jnp.sum(wgt * dwgt, axis=-1, keepdims=True)) / total
        dlogit = dgate * gatev * (1.0 - gatev)
        onehot = (route_rows[..., None] == expert_ids).astype(jnp.float32)
        dfull = jnp.sum(dlogit[..., None] * onehot, axis=1)
        drouter = jnp.dot(dfull, gate_cols.astype(jnp.float32).T, precision=lax.Precision.HIGHEST)
        dnorm = dexp + drouter
        grad_in = (
            grad_f32
            + rscale * dnorm
            - as_f32 * rscale**3 * jnp.mean(dnorm * as_f32, axis=-1, keepdims=True)
        ).astype(jnp.bfloat16)
        passed = from_behind(grad_in, "section", -1)
        return ((passed, new_up, new_down), None)

    start_carry = (
        jnp.zeros((tok_rows, features), jnp.bfloat16),
        jnp.zeros(w_up.shape, jnp.float32),
        jnp.zeros(w_down.shape, jnp.float32),
    )
    final_carry, _ = lax.scan(backward_step, start_carry, jnp.arange(step_count))
    acc_up = final_carry[1]
    acc_down = final_carry[2]
    sum_up, sum_down = lax.psum(
        (acc_up.astype(jnp.bfloat16), acc_down.astype(jnp.bfloat16)), "dp"
    )
    up_out = sum_up.astype(jnp.bfloat16)
    down_out = sum_down.astype(jnp.bfloat16)
    return (up_out[None], down_out[None])


def solution(mesh):
    in_specs = (
        P(None, ("dp", "expert"), None),
        P(None, ("dp", "expert"), None),
        P("section", "expert", None, None),
        P("section", "expert", None, None),
        P("section", None, None),
        P("section", None, ("dp", "expert"), None),
    )
    out_specs = (P("section", "expert", None, None), P("section", "expert", None, None))
    return jax.shard_map(local, mesh=mesh, in_specs=in_specs, out_specs=out_specs, check_vma=False)
```

```python
import functools

import jax
import jax.numpy as jnp
from jax import lax
from jax.experimental import pallas as pl
from jax.experimental.pallas import tpu as pltpu
from jax.sharding import PartitionSpec as P

MESH = pl.DeviceIdType.MESH

CAP = 17


epsilon = 1e-06


def from_behind(block, axis, distance):
    devices = range(lax.axis_size(axis))
    route = [(i - distance, i) for i in devices if i - distance in devices]
    return lax.ppermute(block, axis, route)


def exchange_kernel(n, x_ref, o_ref, copy_sem, send_sem, recv_sem):
    me = lax.axis_index("expert")
    barrier = pltpu.get_barrier_semaphore()
    for j in range(1, n):
        pl.semaphore_signal(
            barrier, inc=1, device_id={"expert": lax.rem(me + j, n)}, device_id_type=MESH
        )
    pl.semaphore_wait(barrier, n - 1)
    local = pltpu.make_async_copy(x_ref.at[me], o_ref.at[me], copy_sem)
    local.start()
    copies = []
    for j in range(1, n):
        peer = lax.rem(me + j, n)
        copy = pltpu.make_async_remote_copy(
            src_ref=x_ref.at[peer],
            dst_ref=o_ref.at[me],
            send_sem=send_sem.at[j],
            recv_sem=recv_sem.at[j],
            device_id={"expert": peer},
            device_id_type=MESH,
        )
        copy.start()
        copies.append(copy)
    local.wait()
    for copy in copies:
        copy.wait()


def expert_exchange(block, site):
    n = block.shape[0]
    nbytes = block.size * block.dtype.itemsize
    return pl.pallas_call(
        functools.partial(exchange_kernel, n),
        out_shape=jax.ShapeDtypeStruct(block.shape, block.dtype),
        in_specs=[pl.BlockSpec(memory_space=pl.ANY)],
        out_specs=pl.BlockSpec(memory_space=pl.ANY),
        scratch_shapes=[
            pltpu.SemaphoreType.DMA(()),
            pltpu.SemaphoreType.DMA((n,)),
            pltpu.SemaphoreType.DMA((n,)),
        ],
        compiler_params=pltpu.CompilerParams(collective_id=site, has_side_effects=True),
        cost_estimate=pl.CostEstimate(flops=0, bytes_accessed=2 * nbytes, transcendentals=0),
    )(block)


def normalize(section_in):
    as_f32 = section_in.astype(jnp.float32)
    rscale = lax.rsqrt(jnp.mean(as_f32 * as_f32, axis=-1, keepdims=True) + epsilon)
    return (as_f32, rscale, (as_f32 * rscale).astype(jnp.bfloat16))


def local(tokens, cotangent, up_proj, down_proj, gate_proj, routes):
    section_pos = lax.axis_index("section")
    section_count = lax.axis_size("section")
    expert_devs = lax.axis_size("expert")
    local_experts = up_proj.shape[1]
    experts_all = local_experts * expert_devs
    micro_count, tok_rows, features = tokens.shape
    top_count = routes.shape[3]
    capacity = CAP
    w_up = up_proj[0]
    w_down = down_proj[0]
    gate_cols = gate_proj[0]
    route_all = routes[0]
    step_count = micro_count + section_count - 1
    expert_ids = jnp.arange(experts_all, dtype=jnp.int32)

    def slot_rows(route_rows):
        flat_ids = route_rows.reshape(-1)
        onehot = (flat_ids[:, None] == expert_ids[None, :]).astype(jnp.int32)
        ranks = jnp.cumsum(onehot, axis=0) - onehot
        slots = jnp.sum(ranks * onehot, axis=1)
        return flat_ids * capacity + slots

    lanes = 128
    pieces = features // lanes

    def slot_sources(dest_rows):
        pair_ids = jnp.arange(dest_rows.shape[0], dtype=jnp.int32)
        return jnp.full((experts_all * capacity,), -1, jnp.int32).at[dest_rows].set(pair_ids)

    dest_all = jax.vmap(slot_rows)(route_all)
    source_all = jax.vmap(slot_sources)(dest_all)

    def to_buffer(row_values, sources, per_row):
        pieces_of = row_values.reshape(-1, pieces, lanes)
        picked = pieces_of[jnp.maximum(sources, 0) // per_row]
        filled = jnp.where((sources >= 0)[:, None, None], picked, jnp.zeros_like(picked))
        return filled.reshape(expert_devs, local_experts * capacity * pieces, lanes)

    def from_buffer(buffer, dest_rows):
        return buffer.reshape(experts_all * capacity, pieces, lanes)[dest_rows].reshape(
            tok_rows, top_count, features
        )

    def as_rows(buffer):
        return buffer.reshape(expert_devs, local_experts, capacity, features)

    def as_pieces(buffer):
        return buffer.reshape(expert_devs, local_experts * capacity * pieces, lanes)

    def gate_values(normed, route_rows):
        logits = jnp.dot(normed, gate_cols, preferred_element_type=jnp.float32)
        return jax.nn.sigmoid(jnp.take_along_axis(logits, route_rows, axis=1))

    def expert_forward(received):
        preact = jnp.einsum("secd,edh->sech", received, w_up, preferred_element_type=jnp.float32)
        hidden = jax.nn.gelu(preact).astype(jnp.bfloat16)
        outbuf = jnp.einsum(
            "sech,ehd->secd", hidden, w_down, preferred_element_type=jnp.float32
        ).astype(jnp.bfloat16)
        return (preact, outbuf)

    def expert_skip(received):
        preact = jnp.zeros(received.shape[:3] + (w_up.shape[2],), jnp.float32)
        return (preact, jnp.zeros_like(received))

    def forward_step(incoming, step_index):
        micro_raw = step_index - section_pos
        live_step = (micro_raw >= 0) & (micro_raw < micro_count)
        micro = jnp.clip(micro_raw, 0, micro_count - 1)
        first_in = lax.dynamic_index_in_dim(tokens, micro, 0, keepdims=False)
        section_in = jnp.where(section_pos == 0, first_in, incoming)
        route_rows = lax.dynamic_index_in_dim(route_all, micro, 0, keepdims=False)
        as_f32, rscale, normed = normalize(section_in)
        gatev = gate_values(normed, route_rows)
        wgt = gatev / jnp.sum(gatev, axis=-1, keepdims=True)
        dest_rows = lax.dynamic_index_in_dim(dest_all, micro, 0, keepdims=False)
        sources = lax.dynamic_index_in_dim(source_all, micro, 0, keepdims=False)
        received = as_rows(expert_exchange(to_buffer(normed, sources, top_count), 3))
        preact, outbuf = lax.cond(live_step, expert_forward, expert_skip, received)
        returned = expert_exchange(as_pieces(outbuf), 0)
        expout = from_buffer(returned, dest_rows)
        section_out = (
            as_f32 + jnp.sum(wgt[..., None] * expout.astype(jnp.float32), axis=1)
        ).astype(jnp.bfloat16)
        passed = from_behind(section_out, "section", 1)
        stored = (section_in, gatev, expout, received, preact)
        return (passed, stored)

    start_act = jnp.zeros((tok_rows, features), jnp.bfloat16)
    _, saved = lax.scan(forward_step, start_act, jnp.arange(step_count))

    def expert_backward(received, dreceived, preact):
        hidden = jax.nn.gelu(preact).astype(jnp.bfloat16)
        down_inc = jnp.einsum(
            "sech,secd->ehd", hidden, dreceived, preferred_element_type=jnp.float32
        )
        dhidden = jnp.einsum(
            "secd,ehd->sech", dreceived, w_down, preferred_element_type=jnp.float32
        )
        _, pullback = jax.vjp(jax.nn.gelu, preact)
        dpre = pullback(dhidden)[0].astype(jnp.bfloat16)
        up_inc = jnp.einsum("secd,sech->edh", received, dpre, preferred_element_type=jnp.float32)
        dinbuf = jnp.einsum(
            "sech,edh->secd", dpre, w_up, preferred_element_type=jnp.float32
        ).astype(jnp.bfloat16)
        return (up_inc, down_inc, dinbuf)

    def backward_skip(operands):
        received, acc_up, acc_down = operands[0], operands[3], operands[4]
        return (acc_up, acc_down, jnp.zeros_like(received))

    def backward_step(carry, step_index):
        incoming, acc_up, acc_down = carry
        micro_raw = step_index - (section_count - 1 - section_pos)
        live_step = (micro_raw >= 0) & (micro_raw < micro_count)
        micro = jnp.clip(micro_raw, 0, micro_count - 1)
        fwd_index = micro + section_pos
        section_in = lax.dynamic_index_in_dim(saved[0], fwd_index, 0, keepdims=False)
        gatev = lax.dynamic_index_in_dim(saved[1], fwd_index, 0, keepdims=False)
        expout = lax.dynamic_index_in_dim(saved[2], fwd_index, 0, keepdims=False)
        last_in = lax.dynamic_index_in_dim(cotangent, micro, 0, keepdims=False)
        grad_out = jnp.where(section_pos == section_count - 1, last_in, incoming)
        route_rows = lax.dynamic_index_in_dim(route_all, micro, 0, keepdims=False)
        dest_rows = lax.dynamic_index_in_dim(dest_all, micro, 0, keepdims=False)
        sources = lax.dynamic_index_in_dim(source_all, micro, 0, keepdims=False)
        as_f32, rscale, normed = normalize(section_in)
        total = jnp.sum(gatev, axis=-1, keepdims=True)
        wgt = gatev / total
        grad_f32 = grad_out.astype(jnp.float32)
        dwgt = jnp.sum(expout.astype(jnp.float32) * grad_f32[:, None, :], axis=-1)
        dout = (
            (wgt[..., None] * grad_f32[:, None, :])
            .astype(jnp.bfloat16)
            .reshape(tok_rows * top_count, features)
        )
        dsend = to_buffer(dout, sources, 1)
        dreceived = as_rows(expert_exchange(dsend, 1))
        received = lax.dynamic_index_in_dim(saved[3], fwd_index, 0, keepdims=False)
        preact = lax.dynamic_index_in_dim(saved[4], fwd_index, 0, keepdims=False)

        def backward_live(operands):
            up_inc, down_inc, dinbuf = expert_backward(operands[0], operands[1], operands[2])
            return (operands[3] + up_inc, operands[4] + down_inc, dinbuf)

        new_up, new_down, dinbuf = lax.cond(
            live_step,
            backward_live,
            backward_skip,
            (received, dreceived, preact, acc_up, acc_down),
        )
        dreturned = expert_exchange(as_pieces(dinbuf), 2)
        dexp = jnp.sum(from_buffer(dreturned, dest_rows).astype(jnp.float32), axis=1)
        dgate = (dwgt - jnp.sum(wgt * dwgt, axis=-1, keepdims=True)) / total
        dlogit = dgate * gatev * (1.0 - gatev)
        onehot = (route_rows[..., None] == expert_ids).astype(jnp.float32)
        dfull = jnp.sum(dlogit[..., None] * onehot, axis=1)
        drouter = jnp.dot(dfull, gate_cols.astype(jnp.float32).T, precision=lax.Precision.HIGHEST)
        dnorm = dexp + drouter
        grad_in = (
            grad_f32
            + rscale * dnorm
            - as_f32 * rscale**3 * jnp.mean(dnorm * as_f32, axis=-1, keepdims=True)
        ).astype(jnp.bfloat16)
        passed = from_behind(grad_in, "section", -1)
        return ((passed, new_up, new_down), None)

    start_carry = (
        jnp.zeros((tok_rows, features), jnp.bfloat16),
        jnp.zeros(w_up.shape, jnp.float32),
        jnp.zeros(w_down.shape, jnp.float32),
    )
    final_carry, _ = lax.scan(backward_step, start_carry, jnp.arange(step_count))
    acc_up = final_carry[1]
    acc_down = final_carry[2]
    sum_up, sum_down = lax.psum(
        (acc_up.astype(jnp.bfloat16), acc_down.astype(jnp.bfloat16)), "dp"
    )
    up_out = sum_up.astype(jnp.bfloat16)
    down_out = sum_down.astype(jnp.bfloat16)
    return (up_out[None], down_out[None])


def solution(mesh):
    in_specs = (
        P(None, ("dp", "expert"), None),
        P(None, ("dp", "expert"), None),
        P("section", "expert", None, None),
        P("section", "expert", None, None),
        P("section", None, None),
        P("section", None, ("dp", "expert"), None),
    )
    out_specs = (P("section", "expert", None, None), P("section", "expert", None, None))
    return jax.shard_map(local, mesh=mesh, in_specs=in_specs, out_specs=out_specs, check_vma=False)
```

```python
import functools

import jax
import jax.numpy as jnp
from jax import lax
from jax.experimental import pallas as pl
from jax.experimental.pallas import tpu as pltpu
from jax.sharding import PartitionSpec as P

MESH = pl.DeviceIdType.MESH

CAP = 17


epsilon = 1e-06


def from_behind(block, axis, distance):
    devices = range(lax.axis_size(axis))
    route = [(i - distance, i) for i in devices if i - distance in devices]
    return lax.ppermute(block, axis, route)


def exchange_kernel(n, x_ref, o_ref, copy_sem, send_sem, recv_sem):
    me = lax.axis_index("expert")
    barrier = pltpu.get_barrier_semaphore()
    for j in range(1, n):
        pl.semaphore_signal(
            barrier, inc=1, device_id={"expert": lax.rem(me + j, n)}, device_id_type=MESH
        )
    pl.semaphore_wait(barrier, n - 1)
    local = pltpu.make_async_copy(x_ref.at[me], o_ref.at[me], copy_sem)
    local.start()
    copies = []
    for j in range(1, n):
        peer = lax.rem(me + j, n)
        copy = pltpu.make_async_remote_copy(
            src_ref=x_ref.at[peer],
            dst_ref=o_ref.at[me],
            send_sem=send_sem.at[j],
            recv_sem=recv_sem.at[j],
            device_id={"expert": peer},
            device_id_type=MESH,
        )
        copy.start()
        copies.append(copy)
    local.wait()
    for copy in copies:
        copy.wait()


def expert_exchange(block, site):
    n = block.shape[0]
    nbytes = block.size * block.dtype.itemsize
    return pl.pallas_call(
        functools.partial(exchange_kernel, n),
        out_shape=jax.ShapeDtypeStruct(block.shape, block.dtype),
        in_specs=[pl.BlockSpec(memory_space=pl.ANY)],
        out_specs=pl.BlockSpec(memory_space=pl.ANY),
        scratch_shapes=[
            pltpu.SemaphoreType.DMA(()),
            pltpu.SemaphoreType.DMA((n,)),
            pltpu.SemaphoreType.DMA((n,)),
        ],
        compiler_params=pltpu.CompilerParams(collective_id=site, has_side_effects=True),
        cost_estimate=pl.CostEstimate(flops=0, bytes_accessed=2 * nbytes, transcendentals=0),
    )(block)


def normalize(section_in):
    as_f32 = section_in.astype(jnp.float32)
    rscale = lax.rsqrt(jnp.mean(as_f32 * as_f32, axis=-1, keepdims=True) + epsilon)
    return (as_f32, rscale, (as_f32 * rscale).astype(jnp.bfloat16))


def local(tokens, cotangent, up_proj, down_proj, gate_proj, routes):
    section_pos = lax.axis_index("section")
    section_count = lax.axis_size("section")
    expert_devs = lax.axis_size("expert")
    local_experts = up_proj.shape[1]
    experts_all = local_experts * expert_devs
    micro_count, tok_rows, features = tokens.shape
    top_count = routes.shape[3]
    capacity = CAP
    w_up = up_proj[0]
    w_down = down_proj[0]
    gate_cols = gate_proj[0]
    route_all = routes[0]
    step_count = micro_count + section_count - 1
    expert_ids = jnp.arange(experts_all, dtype=jnp.int32)

    def slot_rows(route_rows):
        flat_ids = route_rows.reshape(-1)
        onehot = (flat_ids[:, None] == expert_ids[None, :]).astype(jnp.int32)
        ranks = jnp.cumsum(onehot, axis=0) - onehot
        slots = jnp.sum(ranks * onehot, axis=1)
        return flat_ids * capacity + slots

    lanes = 128
    pieces = features // lanes

    def slot_sources(dest_rows):
        pair_ids = jnp.arange(dest_rows.shape[0], dtype=jnp.int32)
        slot_ids = jnp.arange(experts_all * capacity, dtype=jnp.int32)
        hits = dest_rows[:, None] == slot_ids[None, :]
        return jnp.max(jnp.where(hits, pair_ids[:, None], -1), axis=0)

    dest_all = jax.vmap(slot_rows)(route_all)
    source_all = jax.vmap(slot_sources)(dest_all)

    def to_buffer(row_values, sources, per_row):
        pieces_of = row_values.reshape(-1, pieces, lanes)
        picked = pieces_of[jnp.maximum(sources, 0) // per_row]
        filled = jnp.where((sources >= 0)[:, None, None], picked, jnp.zeros_like(picked))
        return filled.reshape(expert_devs, local_experts * capacity * pieces, lanes)

    def from_buffer(buffer, dest_rows):
        return buffer.reshape(experts_all * capacity, pieces, lanes)[dest_rows].reshape(
            tok_rows, top_count, features
        )

    def as_rows(buffer):
        return buffer.reshape(expert_devs, local_experts, capacity, features)

    def as_pieces(buffer):
        return buffer.reshape(expert_devs, local_experts * capacity * pieces, lanes)

    def gate_values(normed, route_rows):
        logits = jnp.dot(normed, gate_cols, preferred_element_type=jnp.float32)
        return jax.nn.sigmoid(jnp.take_along_axis(logits, route_rows, axis=1))

    def expert_forward(received):
        preact = jnp.einsum("secd,edh->sech", received, w_up, preferred_element_type=jnp.float32)
        hidden = jax.nn.gelu(preact).astype(jnp.bfloat16)
        outbuf = jnp.einsum(
            "sech,ehd->secd", hidden, w_down, preferred_element_type=jnp.float32
        ).astype(jnp.bfloat16)
        return (preact, outbuf)

    def expert_skip(received):
        preact = jnp.zeros(received.shape[:3] + (w_up.shape[2],), jnp.float32)
        return (preact, jnp.zeros_like(received))

    def forward_step(incoming, step_index):
        micro_raw = step_index - section_pos
        live_step = (micro_raw >= 0) & (micro_raw < micro_count)
        micro = jnp.clip(micro_raw, 0, micro_count - 1)
        first_in = lax.dynamic_index_in_dim(tokens, micro, 0, keepdims=False)
        section_in = jnp.where(section_pos == 0, first_in, incoming)
        route_rows = lax.dynamic_index_in_dim(route_all, micro, 0, keepdims=False)
        as_f32, rscale, normed = normalize(section_in)
        gatev = gate_values(normed, route_rows)
        wgt = gatev / jnp.sum(gatev, axis=-1, keepdims=True)
        dest_rows = lax.dynamic_index_in_dim(dest_all, micro, 0, keepdims=False)
        sources = lax.dynamic_index_in_dim(source_all, micro, 0, keepdims=False)
        received = as_rows(expert_exchange(to_buffer(normed, sources, top_count), 3))
        preact, outbuf = lax.cond(live_step, expert_forward, expert_skip, received)
        returned = expert_exchange(as_pieces(outbuf), 0)
        expout = from_buffer(returned, dest_rows)
        section_out = (
            as_f32 + jnp.sum(wgt[..., None] * expout.astype(jnp.float32), axis=1)
        ).astype(jnp.bfloat16)
        passed = from_behind(section_out, "section", 1)
        stored = (section_in, gatev, expout, received, preact)
        return (passed, stored)

    start_act = jnp.zeros((tok_rows, features), jnp.bfloat16)
    _, saved = lax.scan(forward_step, start_act, jnp.arange(step_count))

    def expert_backward(dreceived, preact):
        dhidden = jnp.einsum(
            "secd,ehd->sech", dreceived, w_down, preferred_element_type=jnp.float32
        )
        _, pullback = jax.vjp(jax.nn.gelu, preact)
        dpre = pullback(dhidden)[0].astype(jnp.bfloat16)
        dinbuf = jnp.einsum(
            "sech,edh->secd", dpre, w_up, preferred_element_type=jnp.float32
        ).astype(jnp.bfloat16)
        return (dinbuf, dpre, dreceived)

    def backward_skip(operands):
        dreceived, preact = operands
        return (
            jnp.zeros_like(dreceived),
            jnp.zeros(preact.shape, jnp.bfloat16),
            jnp.zeros_like(dreceived),
        )

    def backward_step(incoming, step_index):
        micro_raw = step_index - (section_count - 1 - section_pos)
        live_step = (micro_raw >= 0) & (micro_raw < micro_count)
        micro = jnp.clip(micro_raw, 0, micro_count - 1)
        fwd_index = micro + section_pos
        section_in = lax.dynamic_index_in_dim(saved[0], fwd_index, 0, keepdims=False)
        gatev = lax.dynamic_index_in_dim(saved[1], fwd_index, 0, keepdims=False)
        expout = lax.dynamic_index_in_dim(saved[2], fwd_index, 0, keepdims=False)
        last_in = lax.dynamic_index_in_dim(cotangent, micro, 0, keepdims=False)
        grad_out = jnp.where(section_pos == section_count - 1, last_in, incoming)
        route_rows = lax.dynamic_index_in_dim(route_all, micro, 0, keepdims=False)
        dest_rows = lax.dynamic_index_in_dim(dest_all, micro, 0, keepdims=False)
        sources = lax.dynamic_index_in_dim(source_all, micro, 0, keepdims=False)
        as_f32, rscale, _ = normalize(section_in)
        total = jnp.sum(gatev, axis=-1, keepdims=True)
        wgt = gatev / total
        grad_f32 = grad_out.astype(jnp.float32)
        dwgt = jnp.sum(expout.astype(jnp.float32) * grad_f32[:, None, :], axis=-1)
        dout = (
            (wgt[..., None] * grad_f32[:, None, :])
            .astype(jnp.bfloat16)
            .reshape(tok_rows * top_count, features)
        )
        dsend = to_buffer(dout, sources, 1)
        dreceived = as_rows(expert_exchange(dsend, 1))
        preact = lax.dynamic_index_in_dim(saved[4], fwd_index, 0, keepdims=False)

        def backward_live(operands):
            return expert_backward(operands[0], operands[1])

        dinbuf, dpre, dkept = lax.cond(live_step, backward_live, backward_skip, (dreceived, preact))
        dreturned = expert_exchange(as_pieces(dinbuf), 2)
        dexp = jnp.sum(from_buffer(dreturned, dest_rows).astype(jnp.float32), axis=1)
        dgate = (dwgt - jnp.sum(wgt * dwgt, axis=-1, keepdims=True)) / total
        dlogit = dgate * gatev * (1.0 - gatev)
        onehot = (route_rows[..., None] == expert_ids).astype(jnp.float32)
        dfull = jnp.sum(dlogit[..., None] * onehot, axis=1)
        drouter = jnp.dot(dfull, gate_cols.astype(jnp.float32).T, precision=lax.Precision.HIGHEST)
        dnorm = dexp + drouter
        grad_in = (
            grad_f32
            + rscale * dnorm
            - as_f32 * rscale**3 * jnp.mean(dnorm * as_f32, axis=-1, keepdims=True)
        ).astype(jnp.bfloat16)
        passed = from_behind(grad_in, "section", -1)
        return (passed, (dpre, dkept))

    start_grad = jnp.zeros((tok_rows, features), jnp.bfloat16)
    _, (dpre_all, dreceived_all) = lax.scan(backward_step, start_grad, jnp.arange(step_count))
    back_steps = jnp.arange(step_count)
    fwd_of_back = jnp.clip(back_steps - (section_count - 1 - section_pos), 0, micro_count - 1)
    fwd_of_back = fwd_of_back + section_pos
    received_all = jnp.take(saved[3], fwd_of_back, axis=0)
    hidden_all = jax.nn.gelu(jnp.take(saved[4], fwd_of_back, axis=0)).astype(jnp.bfloat16)
    acc_up = jnp.einsum(
        "bsecd,bsech->edh", received_all, dpre_all, preferred_element_type=jnp.float32
    )
    acc_down = jnp.einsum(
        "bsech,bsecd->ehd", hidden_all, dreceived_all, preferred_element_type=jnp.float32
    )
    sum_up, sum_down = lax.psum(
        (acc_up.astype(jnp.bfloat16), acc_down.astype(jnp.bfloat16)), "dp"
    )
    up_out = sum_up.astype(jnp.bfloat16)
    down_out = sum_down.astype(jnp.bfloat16)
    return (up_out[None], down_out[None])


def solution(mesh):
    in_specs = (
        P(None, ("dp", "expert"), None),
        P(None, ("dp", "expert"), None),
        P("section", "expert", None, None),
        P("section", "expert", None, None),
        P("section", None, None),
        P("section", None, ("dp", "expert"), None),
    )
    out_specs = (P("section", "expert", None, None), P("section", "expert", None, None))
    return jax.shard_map(local, mesh=mesh, in_specs=in_specs, out_specs=out_specs, check_vma=False)
```

```python
import functools

import jax
import jax.numpy as jnp
from jax import lax
from jax.experimental import pallas as pl
from jax.experimental.pallas import tpu as pltpu
from jax.sharding import PartitionSpec as P

MESH = pl.DeviceIdType.MESH

CAP = 17


epsilon = 1e-06


def from_behind(block, axis, distance):
    devices = range(lax.axis_size(axis))
    route = [(i - distance, i) for i in devices if i - distance in devices]
    return lax.ppermute(block, axis, route)


def exchange_kernel(n, x_ref, o_ref, copy_sem, send_sem, recv_sem):
    me = lax.axis_index("expert")
    barrier = pltpu.get_barrier_semaphore()
    for j in range(1, n):
        pl.semaphore_signal(
            barrier, inc=1, device_id={"expert": lax.rem(me + j, n)}, device_id_type=MESH
        )
    pl.semaphore_wait(barrier, n - 1)
    local = pltpu.make_async_copy(x_ref.at[me], o_ref.at[me], copy_sem)
    local.start()
    copies = []
    for j in range(1, n):
        peer = lax.rem(me + j, n)
        copy = pltpu.make_async_remote_copy(
            src_ref=x_ref.at[peer],
            dst_ref=o_ref.at[me],
            send_sem=send_sem.at[j],
            recv_sem=recv_sem.at[j],
            device_id={"expert": peer},
            device_id_type=MESH,
        )
        copy.start()
        copies.append(copy)
    local.wait()
    for copy in copies:
        copy.wait()


def expert_exchange(block, site):
    n = block.shape[0]
    nbytes = block.size * block.dtype.itemsize
    return pl.pallas_call(
        functools.partial(exchange_kernel, n),
        out_shape=jax.ShapeDtypeStruct(block.shape, block.dtype),
        in_specs=[pl.BlockSpec(memory_space=pl.ANY)],
        out_specs=pl.BlockSpec(memory_space=pl.ANY),
        scratch_shapes=[
            pltpu.SemaphoreType.DMA(()),
            pltpu.SemaphoreType.DMA((n,)),
            pltpu.SemaphoreType.DMA((n,)),
        ],
        compiler_params=pltpu.CompilerParams(collective_id=site, has_side_effects=True),
        cost_estimate=pl.CostEstimate(flops=0, bytes_accessed=2 * nbytes, transcendentals=0),
    )(block)


def normalize(section_in):
    as_f32 = section_in.astype(jnp.float32)
    rscale = lax.rsqrt(jnp.mean(as_f32 * as_f32, axis=-1, keepdims=True) + epsilon)
    return (as_f32, rscale, (as_f32 * rscale).astype(jnp.bfloat16))


def local(tokens, cotangent, up_proj, down_proj, gate_proj, routes):
    section_pos = lax.axis_index("section")
    section_count = lax.axis_size("section")
    expert_devs = lax.axis_size("expert")
    local_experts = up_proj.shape[1]
    experts_all = local_experts * expert_devs
    micro_count, tok_rows, features = tokens.shape
    top_count = routes.shape[3]
    capacity = CAP
    w_up = up_proj[0]
    w_down = down_proj[0]
    gate_cols = gate_proj[0]
    route_all = routes[0]
    step_count = micro_count + section_count - 1
    expert_ids = jnp.arange(experts_all, dtype=jnp.int32)

    def slot_rows(route_rows):
        flat_ids = route_rows.reshape(-1)
        onehot = (flat_ids[:, None] == expert_ids[None, :]).astype(jnp.int32)
        ranks = jnp.cumsum(onehot, axis=0) - onehot
        slots = jnp.sum(ranks * onehot, axis=1)
        return flat_ids * capacity + slots

    lanes = 128
    pieces = features // lanes

    def slot_sources(dest_rows):
        pair_ids = jnp.arange(dest_rows.shape[0], dtype=jnp.int32)
        slot_ids = jnp.arange(experts_all * capacity, dtype=jnp.int32)
        hits = dest_rows[:, None] == slot_ids[None, :]
        return jnp.max(jnp.where(hits, pair_ids[:, None], -1), axis=0)

    dest_all = jax.vmap(slot_rows)(route_all)
    source_all = jax.vmap(slot_sources)(dest_all)

    def to_buffer(row_values, sources, per_row):
        pieces_of = row_values.reshape(-1, pieces, lanes)
        picked = pieces_of[jnp.maximum(sources, 0) // per_row]
        filled = jnp.where((sources >= 0)[:, None, None], picked, jnp.zeros_like(picked))
        return filled.reshape(expert_devs, local_experts * capacity * pieces, lanes)

    def from_buffer(buffer, dest_rows):
        return buffer.reshape(experts_all * capacity, pieces, lanes)[dest_rows].reshape(
            tok_rows, top_count, features
        )

    def as_rows(buffer):
        return buffer.reshape(expert_devs, local_experts, capacity, features)

    def as_pieces(buffer):
        return buffer.reshape(expert_devs, local_experts * capacity * pieces, lanes)

    def gate_values(normed, route_rows):
        logits = jnp.dot(normed, gate_cols, preferred_element_type=jnp.float32)
        return jax.nn.sigmoid(jnp.take_along_axis(logits, route_rows, axis=1))

    def expert_forward(received):
        preact = jnp.einsum("secd,edh->sech", received, w_up, preferred_element_type=jnp.float32)
        hidden = jax.nn.gelu(preact).astype(jnp.bfloat16)
        outbuf = jnp.einsum(
            "sech,ehd->secd", hidden, w_down, preferred_element_type=jnp.float32
        ).astype(jnp.bfloat16)
        return (preact, outbuf)

    def expert_skip(received):
        preact = jnp.zeros(received.shape[:3] + (w_up.shape[2],), jnp.float32)
        return (preact, jnp.zeros_like(received))

    def forward_step(incoming, step_index):
        micro_raw = step_index - section_pos
        live_step = (micro_raw >= 0) & (micro_raw < micro_count)
        micro = jnp.clip(micro_raw, 0, micro_count - 1)
        first_in = lax.dynamic_index_in_dim(tokens, micro, 0, keepdims=False)
        section_in = jnp.where(section_pos == 0, first_in, incoming)
        route_rows = lax.dynamic_index_in_dim(route_all, micro, 0, keepdims=False)
        as_f32, rscale, normed = normalize(section_in)
        gatev = gate_values(normed, route_rows)
        wgt = gatev / jnp.sum(gatev, axis=-1, keepdims=True)
        dest_rows = lax.dynamic_index_in_dim(dest_all, micro, 0, keepdims=False)
        sources = lax.dynamic_index_in_dim(source_all, micro, 0, keepdims=False)
        received = as_rows(expert_exchange(to_buffer(normed, sources, top_count), 3))
        preact, outbuf = lax.cond(live_step, expert_forward, expert_skip, received)
        returned = expert_exchange(as_pieces(outbuf), 0)
        expout = from_buffer(returned, dest_rows)
        section_out = (
            as_f32 + jnp.sum(wgt[..., None] * expout.astype(jnp.float32), axis=1)
        ).astype(jnp.bfloat16)
        passed = from_behind(section_out, "section", 1)
        stored = (section_in, gatev, expout, received, preact)
        return (passed, stored)

    start_act = jnp.zeros((tok_rows, features), jnp.bfloat16)
    _, saved = lax.scan(forward_step, start_act, jnp.arange(step_count))

    def expert_backward(dreceived, preact):
        dhidden = jnp.einsum(
            "secd,ehd->sech", dreceived, w_down, preferred_element_type=jnp.float32
        )
        _, pullback = jax.vjp(jax.nn.gelu, preact)
        dpre = pullback(dhidden)[0].astype(jnp.bfloat16)
        dinbuf = jnp.einsum(
            "sech,edh->secd", dpre, w_up, preferred_element_type=jnp.float32
        ).astype(jnp.bfloat16)
        return (dinbuf, dpre, dreceived)

    def backward_skip(operands):
        dreceived, preact = operands
        return (
            jnp.zeros_like(dreceived),
            jnp.zeros(preact.shape, jnp.bfloat16),
            jnp.zeros_like(dreceived),
        )

    def backward_step(incoming, step_index):
        micro_raw = step_index - (section_count - 1 - section_pos)
        live_step = (micro_raw >= 0) & (micro_raw < micro_count)
        micro = jnp.clip(micro_raw, 0, micro_count - 1)
        fwd_index = micro + section_pos
        section_in = lax.dynamic_index_in_dim(saved[0], fwd_index, 0, keepdims=False)
        gatev = lax.dynamic_index_in_dim(saved[1], fwd_index, 0, keepdims=False)
        expout = lax.dynamic_index_in_dim(saved[2], fwd_index, 0, keepdims=False)
        last_in = lax.dynamic_index_in_dim(cotangent, micro, 0, keepdims=False)
        grad_out = jnp.where(section_pos == section_count - 1, last_in, incoming)
        route_rows = lax.dynamic_index_in_dim(route_all, micro, 0, keepdims=False)
        dest_rows = lax.dynamic_index_in_dim(dest_all, micro, 0, keepdims=False)
        sources = lax.dynamic_index_in_dim(source_all, micro, 0, keepdims=False)
        as_f32, rscale, _ = normalize(section_in)
        total = jnp.sum(gatev, axis=-1, keepdims=True)
        wgt = gatev / total
        grad_f32 = grad_out.astype(jnp.float32)
        dwgt = jnp.sum(expout.astype(jnp.float32) * grad_f32[:, None, :], axis=-1)
        dout = (
            (wgt[..., None] * grad_f32[:, None, :])
            .astype(jnp.bfloat16)
            .reshape(tok_rows * top_count, features)
        )
        dsend = to_buffer(dout, sources, 1)
        dreceived = as_rows(expert_exchange(dsend, 1))
        preact = lax.dynamic_index_in_dim(saved[4], fwd_index, 0, keepdims=False)

        def backward_live(operands):
            return expert_backward(operands[0], operands[1])

        dinbuf, dpre, dkept = lax.cond(live_step, backward_live, backward_skip, (dreceived, preact))
        dreturned = expert_exchange(as_pieces(dinbuf), 2)
        dexp = jnp.sum(from_buffer(dreturned, dest_rows).astype(jnp.float32), axis=1)
        dgate = (dwgt - jnp.sum(wgt * dwgt, axis=-1, keepdims=True)) / total
        dlogit = dgate * gatev * (1.0 - gatev)
        onehot = (route_rows[..., None] == expert_ids).astype(jnp.float32)
        dfull = jnp.sum(dlogit[..., None] * onehot, axis=1)
        drouter = jnp.dot(dfull, gate_cols.astype(jnp.float32).T, precision=lax.Precision.HIGHEST)
        dnorm = dexp + drouter
        grad_in = (
            grad_f32
            + rscale * dnorm
            - as_f32 * rscale**3 * jnp.mean(dnorm * as_f32, axis=-1, keepdims=True)
        ).astype(jnp.bfloat16)
        passed = from_behind(grad_in, "section", -1)
        return (passed, (dpre, dkept))

    start_grad = jnp.zeros((tok_rows, features), jnp.bfloat16)
    _, (dpre_all, dreceived_all) = lax.scan(backward_step, start_grad, jnp.arange(step_count))
    first_back = section_count - 1 - section_pos
    dpre_live = lax.dynamic_slice_in_dim(dpre_all, first_back, micro_count, axis=0)
    dreceived_live = lax.dynamic_slice_in_dim(dreceived_all, first_back, micro_count, axis=0)
    received_live = lax.dynamic_slice_in_dim(saved[3], section_pos, micro_count, axis=0)
    preact_live = lax.dynamic_slice_in_dim(saved[4], section_pos, micro_count, axis=0)
    hidden_live = jax.nn.gelu(preact_live).astype(jnp.bfloat16)
    acc_up = jnp.einsum(
        "bsecd,bsech->edh", received_live, dpre_live, preferred_element_type=jnp.float32
    )
    sum_up = lax.psum(acc_up.astype(jnp.bfloat16), "dp")
    acc_down = jnp.einsum(
        "bsech,bsecd->ehd", hidden_live, dreceived_live, preferred_element_type=jnp.float32
    )
    sum_down = lax.psum(acc_down.astype(jnp.bfloat16), "dp")
    up_out = sum_up.astype(jnp.bfloat16)
    down_out = sum_down.astype(jnp.bfloat16)
    return (up_out[None], down_out[None])


def solution(mesh):
    in_specs = (
        P(None, ("dp", "expert"), None),
        P(None, ("dp", "expert"), None),
        P("section", "expert", None, None),
        P("section", "expert", None, None),
        P("section", None, None),
        P("section", None, ("dp", "expert"), None),
    )
    out_specs = (P("section", "expert", None, None), P("section", "expert", None, None))
    return jax.shard_map(local, mesh=mesh, in_specs=in_specs, out_specs=out_specs, check_vma=False)
```

```python
import functools

import jax
import jax.numpy as jnp
from jax import lax
from jax.experimental import pallas as pl
from jax.experimental.pallas import tpu as pltpu
from jax.sharding import PartitionSpec as P

MESH = pl.DeviceIdType.MESH

CAP = 17


epsilon = 1e-06


def from_behind(block, axis, distance):
    devices = range(lax.axis_size(axis))
    route = [(i - distance, i) for i in devices if i - distance in devices]
    return lax.ppermute(block, axis, route)


def exchange_kernel(n, x_ref, o_ref, copy_sem, send_sem, recv_sem):
    me = lax.axis_index("expert")
    barrier = pltpu.get_barrier_semaphore()
    for j in range(1, n):
        pl.semaphore_signal(
            barrier, inc=1, device_id={"expert": lax.rem(me + j, n)}, device_id_type=MESH
        )
    pl.semaphore_wait(barrier, n - 1)
    local = pltpu.make_async_copy(x_ref.at[me], o_ref.at[me], copy_sem)
    local.start()
    copies = []
    for j in range(1, n):
        peer = lax.rem(me + j, n)
        copy = pltpu.make_async_remote_copy(
            src_ref=x_ref.at[peer],
            dst_ref=o_ref.at[me],
            send_sem=send_sem.at[j],
            recv_sem=recv_sem.at[j],
            device_id={"expert": peer},
            device_id_type=MESH,
        )
        copy.start()
        copies.append(copy)
    local.wait()
    for copy in copies:
        copy.wait()


def expert_exchange(block, site):
    n = block.shape[0]
    nbytes = block.size * block.dtype.itemsize
    return pl.pallas_call(
        functools.partial(exchange_kernel, n),
        out_shape=jax.ShapeDtypeStruct(block.shape, block.dtype),
        in_specs=[pl.BlockSpec(memory_space=pl.ANY)],
        out_specs=pl.BlockSpec(memory_space=pl.ANY),
        scratch_shapes=[
            pltpu.SemaphoreType.DMA(()),
            pltpu.SemaphoreType.DMA((n,)),
            pltpu.SemaphoreType.DMA((n,)),
        ],
        compiler_params=pltpu.CompilerParams(collective_id=site, has_side_effects=True),
        cost_estimate=pl.CostEstimate(flops=0, bytes_accessed=2 * nbytes, transcendentals=0),
    )(block)


def ring_sum(flat, axis):
    count = lax.axis_size(axis)
    me = lax.axis_index(axis)
    halves = flat.reshape(2, count, -1, 128)
    results = []
    for half, way in ((0, 1), (1, -1)):
        own = halves[half]
        route = [(i, (i + way) % count) for i in range(count)]
        send = lax.dynamic_index_in_dim(own, me, 0, keepdims=False).astype(jnp.bfloat16)
        for step in range(count - 1):
            got = lax.ppermute(send, axis, route)
            chunk = lax.rem(me - way * (1 + step) + 2 * count, count)
            part = lax.dynamic_index_in_dim(own, chunk, 0, keepdims=False)
            send = (got.astype(jnp.float32) + part).astype(jnp.bfloat16)
        out = jnp.zeros(own.shape, jnp.bfloat16)
        out = lax.dynamic_update_index_in_dim(out, send, lax.rem(me + way + count, count), 0)
        for step in range(count - 1):
            send = lax.ppermute(send, axis, route)
            chunk = lax.rem(me - way * step + 2 * count, count)
            out = lax.dynamic_update_index_in_dim(out, send, chunk, 0)
        results.append(out.reshape(-1))
    return jnp.concatenate(results)


def normalize(section_in):
    as_f32 = section_in.astype(jnp.float32)
    rscale = lax.rsqrt(jnp.mean(as_f32 * as_f32, axis=-1, keepdims=True) + epsilon)
    return (as_f32, rscale, (as_f32 * rscale).astype(jnp.bfloat16))


def local(tokens, cotangent, up_proj, down_proj, gate_proj, routes):
    section_pos = lax.axis_index("section")
    section_count = lax.axis_size("section")
    expert_devs = lax.axis_size("expert")
    local_experts = up_proj.shape[1]
    experts_all = local_experts * expert_devs
    micro_count, tok_rows, features = tokens.shape
    top_count = routes.shape[3]
    capacity = CAP
    w_up = up_proj[0]
    w_down = down_proj[0]
    gate_cols = gate_proj[0]
    route_all = routes[0]
    step_count = micro_count + section_count - 1
    expert_ids = jnp.arange(experts_all, dtype=jnp.int32)

    def slot_rows(route_rows):
        flat_ids = route_rows.reshape(-1)
        onehot = (flat_ids[:, None] == expert_ids[None, :]).astype(jnp.int32)
        ranks = jnp.cumsum(onehot, axis=0) - onehot
        slots = jnp.sum(ranks * onehot, axis=1)
        return flat_ids * capacity + slots

    lanes = 128
    pieces = features // lanes

    def slot_sources(dest_rows):
        pair_ids = jnp.arange(dest_rows.shape[0], dtype=jnp.int32)
        slot_ids = jnp.arange(experts_all * capacity, dtype=jnp.int32)
        hits = dest_rows[:, None] == slot_ids[None, :]
        return jnp.max(jnp.where(hits, pair_ids[:, None], -1), axis=0)

    dest_all = jax.vmap(slot_rows)(route_all)
    source_all = jax.vmap(slot_sources)(dest_all)

    def to_buffer(row_values, sources, per_row):
        pieces_of = row_values.reshape(-1, pieces, lanes)
        picked = pieces_of[jnp.maximum(sources, 0) // per_row]
        filled = jnp.where((sources >= 0)[:, None, None], picked, jnp.zeros_like(picked))
        return filled.reshape(expert_devs, local_experts * capacity * pieces, lanes)

    def from_buffer(buffer, dest_rows):
        return buffer.reshape(experts_all * capacity, pieces, lanes)[dest_rows].reshape(
            tok_rows, top_count, features
        )

    def as_rows(buffer):
        return buffer.reshape(expert_devs, local_experts, capacity, features)

    def as_pieces(buffer):
        return buffer.reshape(expert_devs, local_experts * capacity * pieces, lanes)

    def gate_values(normed, route_rows):
        logits = jnp.dot(normed, gate_cols, preferred_element_type=jnp.float32)
        return jax.nn.sigmoid(jnp.take_along_axis(logits, route_rows, axis=1))

    def expert_forward(received):
        preact = jnp.einsum("secd,edh->sech", received, w_up, preferred_element_type=jnp.float32)
        hidden = jax.nn.gelu(preact).astype(jnp.bfloat16)
        outbuf = jnp.einsum(
            "sech,ehd->secd", hidden, w_down, preferred_element_type=jnp.float32
        ).astype(jnp.bfloat16)
        return (preact, outbuf)

    def expert_skip(received):
        preact = jnp.zeros(received.shape[:3] + (w_up.shape[2],), jnp.float32)
        return (preact, jnp.zeros_like(received))

    def forward_step(incoming, step_index):
        micro_raw = step_index - section_pos
        live_step = (micro_raw >= 0) & (micro_raw < micro_count)
        micro = jnp.clip(micro_raw, 0, micro_count - 1)
        first_in = lax.dynamic_index_in_dim(tokens, micro, 0, keepdims=False)
        section_in = jnp.where(section_pos == 0, first_in, incoming)
        route_rows = lax.dynamic_index_in_dim(route_all, micro, 0, keepdims=False)
        as_f32, rscale, normed = normalize(section_in)
        gatev = gate_values(normed, route_rows)
        wgt = gatev / jnp.sum(gatev, axis=-1, keepdims=True)
        dest_rows = lax.dynamic_index_in_dim(dest_all, micro, 0, keepdims=False)
        sources = lax.dynamic_index_in_dim(source_all, micro, 0, keepdims=False)
        received = as_rows(expert_exchange(to_buffer(normed, sources, top_count), 3))
        preact, outbuf = lax.cond(live_step, expert_forward, expert_skip, received)
        returned = expert_exchange(as_pieces(outbuf), 0)
        expout = from_buffer(returned, dest_rows)
        section_out = (
            as_f32 + jnp.sum(wgt[..., None] * expout.astype(jnp.float32), axis=1)
        ).astype(jnp.bfloat16)
        passed = from_behind(section_out, "section", 1)
        stored = (section_in, gatev, expout, received, preact)
        return (passed, stored)

    start_act = jnp.zeros((tok_rows, features), jnp.bfloat16)
    _, saved = lax.scan(forward_step, start_act, jnp.arange(step_count))

    def expert_backward(dreceived, preact):
        dhidden = jnp.einsum(
            "secd,ehd->sech", dreceived, w_down, preferred_element_type=jnp.float32
        )
        _, pullback = jax.vjp(jax.nn.gelu, preact)
        dpre = pullback(dhidden)[0].astype(jnp.bfloat16)
        dinbuf = jnp.einsum(
            "sech,edh->secd", dpre, w_up, preferred_element_type=jnp.float32
        ).astype(jnp.bfloat16)
        return (dinbuf, dpre, dreceived)

    def backward_skip(operands):
        dreceived, preact = operands
        return (
            jnp.zeros_like(dreceived),
            jnp.zeros(preact.shape, jnp.bfloat16),
            jnp.zeros_like(dreceived),
        )

    def backward_step(incoming, step_index):
        micro_raw = step_index - (section_count - 1 - section_pos)
        live_step = (micro_raw >= 0) & (micro_raw < micro_count)
        micro = jnp.clip(micro_raw, 0, micro_count - 1)
        fwd_index = micro + section_pos
        section_in = lax.dynamic_index_in_dim(saved[0], fwd_index, 0, keepdims=False)
        gatev = lax.dynamic_index_in_dim(saved[1], fwd_index, 0, keepdims=False)
        expout = lax.dynamic_index_in_dim(saved[2], fwd_index, 0, keepdims=False)
        last_in = lax.dynamic_index_in_dim(cotangent, micro, 0, keepdims=False)
        grad_out = jnp.where(section_pos == section_count - 1, last_in, incoming)
        route_rows = lax.dynamic_index_in_dim(route_all, micro, 0, keepdims=False)
        dest_rows = lax.dynamic_index_in_dim(dest_all, micro, 0, keepdims=False)
        sources = lax.dynamic_index_in_dim(source_all, micro, 0, keepdims=False)
        as_f32, rscale, _ = normalize(section_in)
        total = jnp.sum(gatev, axis=-1, keepdims=True)
        wgt = gatev / total
        grad_f32 = grad_out.astype(jnp.float32)
        dwgt = jnp.sum(expout.astype(jnp.float32) * grad_f32[:, None, :], axis=-1)
        dout = (
            (wgt[..., None] * grad_f32[:, None, :])
            .astype(jnp.bfloat16)
            .reshape(tok_rows * top_count, features)
        )
        dsend = to_buffer(dout, sources, 1)
        dreceived = as_rows(expert_exchange(dsend, 1))
        preact = lax.dynamic_index_in_dim(saved[4], fwd_index, 0, keepdims=False)

        def backward_live(operands):
            return expert_backward(operands[0], operands[1])

        dinbuf, dpre, dkept = lax.cond(live_step, backward_live, backward_skip, (dreceived, preact))
        dreturned = expert_exchange(as_pieces(dinbuf), 2)
        dexp = jnp.sum(from_buffer(dreturned, dest_rows).astype(jnp.float32), axis=1)
        dgate = (dwgt - jnp.sum(wgt * dwgt, axis=-1, keepdims=True)) / total
        dlogit = dgate * gatev * (1.0 - gatev)
        onehot = (route_rows[..., None] == expert_ids).astype(jnp.float32)
        dfull = jnp.sum(dlogit[..., None] * onehot, axis=1)
        drouter = jnp.dot(dfull, gate_cols.astype(jnp.float32).T, precision=lax.Precision.HIGHEST)
        dnorm = dexp + drouter
        grad_in = (
            grad_f32
            + rscale * dnorm
            - as_f32 * rscale**3 * jnp.mean(dnorm * as_f32, axis=-1, keepdims=True)
        ).astype(jnp.bfloat16)
        passed = from_behind(grad_in, "section", -1)
        return (passed, (dpre, dkept))

    start_grad = jnp.zeros((tok_rows, features), jnp.bfloat16)
    _, (dpre_all, dreceived_all) = lax.scan(backward_step, start_grad, jnp.arange(step_count))
    first_back = section_count - 1 - section_pos
    dpre_live = lax.dynamic_slice_in_dim(dpre_all, first_back, micro_count, axis=0)
    dreceived_live = lax.dynamic_slice_in_dim(dreceived_all, first_back, micro_count, axis=0)
    received_live = lax.dynamic_slice_in_dim(saved[3], section_pos, micro_count, axis=0)
    preact_live = lax.dynamic_slice_in_dim(saved[4], section_pos, micro_count, axis=0)
    hidden_live = jax.nn.gelu(preact_live).astype(jnp.bfloat16)
    acc_up = jnp.einsum(
        "bsecd,bsech->edh", received_live, dpre_live, preferred_element_type=jnp.float32
    )
    acc_down = jnp.einsum(
        "bsech,bsecd->ehd", hidden_live, dreceived_live, preferred_element_type=jnp.float32
    )
    summed = ring_sum(jnp.concatenate([acc_up.reshape(-1), acc_down.reshape(-1)]), "dp")
    sum_up = summed[: acc_up.size].reshape(acc_up.shape)
    sum_down = summed[acc_up.size :].reshape(acc_down.shape)
    up_out = sum_up.astype(jnp.bfloat16)
    down_out = sum_down.astype(jnp.bfloat16)
    return (up_out[None], down_out[None])


def solution(mesh):
    in_specs = (
        P(None, ("dp", "expert"), None),
        P(None, ("dp", "expert"), None),
        P("section", "expert", None, None),
        P("section", "expert", None, None),
        P("section", None, None),
        P("section", None, ("dp", "expert"), None),
    )
    out_specs = (P("section", "expert", None, None), P("section", "expert", None, None))
    return jax.shard_map(local, mesh=mesh, in_specs=in_specs, out_specs=out_specs, check_vma=False)
```

```python
import functools

import jax
import jax.numpy as jnp
from jax import lax
from jax.experimental import pallas as pl
from jax.experimental.pallas import tpu as pltpu
from jax.sharding import PartitionSpec as P

MESH = pl.DeviceIdType.MESH

CAP = 17


epsilon = 1e-06


def from_behind(block, axis, distance):
    devices = range(lax.axis_size(axis))
    route = [(i - distance, i) for i in devices if i - distance in devices]
    return lax.ppermute(block, axis, route)


def exchange_kernel(n, x_ref, o_ref, copy_sem, send_sem, recv_sem):
    me = lax.axis_index("expert")
    barrier = pltpu.get_barrier_semaphore()
    for j in range(1, n):
        pl.semaphore_signal(
            barrier, inc=1, device_id={"expert": lax.rem(me + j, n)}, device_id_type=MESH
        )
    pl.semaphore_wait(barrier, n - 1)
    local = pltpu.make_async_copy(x_ref.at[me], o_ref.at[me], copy_sem)
    local.start()
    copies = []
    for j in range(1, n):
        peer = lax.rem(me + j, n)
        copy = pltpu.make_async_remote_copy(
            src_ref=x_ref.at[peer],
            dst_ref=o_ref.at[me],
            send_sem=send_sem.at[j],
            recv_sem=recv_sem.at[j],
            device_id={"expert": peer},
            device_id_type=MESH,
        )
        copy.start()
        copies.append(copy)
    local.wait()
    for copy in copies:
        copy.wait()


def expert_exchange(block, site):
    n = block.shape[0]
    nbytes = block.size * block.dtype.itemsize
    return pl.pallas_call(
        functools.partial(exchange_kernel, n),
        out_shape=jax.ShapeDtypeStruct(block.shape, block.dtype),
        in_specs=[pl.BlockSpec(memory_space=pl.ANY)],
        out_specs=pl.BlockSpec(memory_space=pl.ANY),
        scratch_shapes=[
            pltpu.SemaphoreType.DMA(()),
            pltpu.SemaphoreType.DMA((n,)),
            pltpu.SemaphoreType.DMA((n,)),
        ],
        compiler_params=pltpu.CompilerParams(collective_id=site, has_side_effects=True),
        cost_estimate=pl.CostEstimate(flops=0, bytes_accessed=2 * nbytes, transcendentals=0),
    )(block)


def ring_sum(flat, axis):
    count = lax.axis_size(axis)
    me = lax.axis_index(axis)
    halves = flat.reshape(2, count, -1, flat.shape[-1])
    results = []
    for half, way in ((0, 1), (1, -1)):
        own = halves[half]
        route = [(i, (i + way) % count) for i in range(count)]
        send = lax.dynamic_index_in_dim(own, me, 0, keepdims=False).astype(jnp.bfloat16)
        for step in range(count - 1):
            got = lax.ppermute(send, axis, route)
            chunk = lax.rem(me - way * (1 + step) + 2 * count, count)
            part = lax.dynamic_index_in_dim(own, chunk, 0, keepdims=False)
            send = (got.astype(jnp.float32) + part).astype(jnp.bfloat16)
        out = jnp.zeros(own.shape, jnp.bfloat16)
        out = lax.dynamic_update_index_in_dim(out, send, lax.rem(me + way + count, count), 0)
        for step in range(count - 1):
            send = lax.ppermute(send, axis, route)
            chunk = lax.rem(me - way * step + 2 * count, count)
            out = lax.dynamic_update_index_in_dim(out, send, chunk, 0)
        results.append(out)
    return jnp.stack(results).reshape(flat.shape)


def normalize(section_in):
    as_f32 = section_in.astype(jnp.float32)
    rscale = lax.rsqrt(jnp.mean(as_f32 * as_f32, axis=-1, keepdims=True) + epsilon)
    return (as_f32, rscale, (as_f32 * rscale).astype(jnp.bfloat16))


def local(tokens, cotangent, up_proj, down_proj, gate_proj, routes):
    section_pos = lax.axis_index("section")
    section_count = lax.axis_size("section")
    expert_devs = lax.axis_size("expert")
    local_experts = up_proj.shape[1]
    experts_all = local_experts * expert_devs
    micro_count, tok_rows, features = tokens.shape
    top_count = routes.shape[3]
    capacity = CAP
    w_up = up_proj[0]
    w_down = down_proj[0]
    gate_cols = gate_proj[0]
    route_all = routes[0]
    step_count = micro_count + section_count - 1
    expert_ids = jnp.arange(experts_all, dtype=jnp.int32)

    def slot_rows(route_rows):
        flat_ids = route_rows.reshape(-1)
        onehot = (flat_ids[:, None] == expert_ids[None, :]).astype(jnp.int32)
        ranks = jnp.cumsum(onehot, axis=0) - onehot
        slots = jnp.sum(ranks * onehot, axis=1)
        return flat_ids * capacity + slots

    lanes = 128
    pieces = features // lanes

    def slot_sources(dest_rows):
        pair_ids = jnp.arange(dest_rows.shape[0], dtype=jnp.int32)
        slot_ids = jnp.arange(experts_all * capacity, dtype=jnp.int32)
        hits = dest_rows[:, None] == slot_ids[None, :]
        return jnp.max(jnp.where(hits, pair_ids[:, None], -1), axis=0)

    dest_all = jax.vmap(slot_rows)(route_all)
    source_all = jax.vmap(slot_sources)(dest_all)

    def to_buffer(row_values, sources, per_row):
        pieces_of = row_values.reshape(-1, pieces, lanes)
        picked = pieces_of[jnp.maximum(sources, 0) // per_row]
        filled = jnp.where((sources >= 0)[:, None, None], picked, jnp.zeros_like(picked))
        return filled.reshape(expert_devs, local_experts * capacity * pieces, lanes)

    def from_buffer(buffer, dest_rows):
        return buffer.reshape(experts_all * capacity, pieces, lanes)[dest_rows].reshape(
            tok_rows, top_count, features
        )

    def as_rows(buffer):
        return buffer.reshape(expert_devs, local_experts, capacity, features)

    def as_pieces(buffer):
        return buffer.reshape(expert_devs, local_experts * capacity * pieces, lanes)

    def gate_values(normed, route_rows):
        logits = jnp.dot(normed, gate_cols, preferred_element_type=jnp.float32)
        return jax.nn.sigmoid(jnp.take_along_axis(logits, route_rows, axis=1))

    def expert_forward(received):
        preact = jnp.einsum("secd,edh->sech", received, w_up, preferred_element_type=jnp.float32)
        hidden = jax.nn.gelu(preact).astype(jnp.bfloat16)
        outbuf = jnp.einsum(
            "sech,ehd->secd", hidden, w_down, preferred_element_type=jnp.float32
        ).astype(jnp.bfloat16)
        return (preact, outbuf)

    def expert_skip(received):
        preact = jnp.zeros(received.shape[:3] + (w_up.shape[2],), jnp.float32)
        return (preact, jnp.zeros_like(received))

    def forward_step(incoming, step_index):
        micro_raw = step_index - section_pos
        live_step = (micro_raw >= 0) & (micro_raw < micro_count)
        micro = jnp.clip(micro_raw, 0, micro_count - 1)
        first_in = lax.dynamic_index_in_dim(tokens, micro, 0, keepdims=False)
        section_in = jnp.where(section_pos == 0, first_in, incoming)
        route_rows = lax.dynamic_index_in_dim(route_all, micro, 0, keepdims=False)
        as_f32, rscale, normed = normalize(section_in)
        gatev = gate_values(normed, route_rows)
        wgt = gatev / jnp.sum(gatev, axis=-1, keepdims=True)
        dest_rows = lax.dynamic_index_in_dim(dest_all, micro, 0, keepdims=False)
        sources = lax.dynamic_index_in_dim(source_all, micro, 0, keepdims=False)
        received = as_rows(expert_exchange(to_buffer(normed, sources, top_count), 3))
        preact, outbuf = lax.cond(live_step, expert_forward, expert_skip, received)
        returned = expert_exchange(as_pieces(outbuf), 0)
        expout = from_buffer(returned, dest_rows)
        section_out = (
            as_f32 + jnp.sum(wgt[..., None] * expout.astype(jnp.float32), axis=1)
        ).astype(jnp.bfloat16)
        passed = from_behind(section_out, "section", 1)
        stored = (section_in, gatev, expout, received, preact)
        return (passed, stored)

    start_act = jnp.zeros((tok_rows, features), jnp.bfloat16)
    _, saved = lax.scan(forward_step, start_act, jnp.arange(step_count))

    def expert_backward(dreceived, preact):
        dhidden = jnp.einsum(
            "secd,ehd->sech", dreceived, w_down, preferred_element_type=jnp.float32
        )
        _, pullback = jax.vjp(jax.nn.gelu, preact)
        dpre = pullback(dhidden)[0].astype(jnp.bfloat16)
        dinbuf = jnp.einsum(
            "sech,edh->secd", dpre, w_up, preferred_element_type=jnp.float32
        ).astype(jnp.bfloat16)
        return (dinbuf, dpre, dreceived)

    def backward_skip(operands):
        dreceived, preact = operands
        return (
            jnp.zeros_like(dreceived),
            jnp.zeros(preact.shape, jnp.bfloat16),
            jnp.zeros_like(dreceived),
        )

    def backward_step(incoming, step_index):
        micro_raw = step_index - (section_count - 1 - section_pos)
        live_step = (micro_raw >= 0) & (micro_raw < micro_count)
        micro = jnp.clip(micro_raw, 0, micro_count - 1)
        fwd_index = micro + section_pos
        section_in = lax.dynamic_index_in_dim(saved[0], fwd_index, 0, keepdims=False)
        gatev = lax.dynamic_index_in_dim(saved[1], fwd_index, 0, keepdims=False)
        expout = lax.dynamic_index_in_dim(saved[2], fwd_index, 0, keepdims=False)
        last_in = lax.dynamic_index_in_dim(cotangent, micro, 0, keepdims=False)
        grad_out = jnp.where(section_pos == section_count - 1, last_in, incoming)
        route_rows = lax.dynamic_index_in_dim(route_all, micro, 0, keepdims=False)
        dest_rows = lax.dynamic_index_in_dim(dest_all, micro, 0, keepdims=False)
        sources = lax.dynamic_index_in_dim(source_all, micro, 0, keepdims=False)
        as_f32, rscale, _ = normalize(section_in)
        total = jnp.sum(gatev, axis=-1, keepdims=True)
        wgt = gatev / total
        grad_f32 = grad_out.astype(jnp.float32)
        dwgt = jnp.sum(expout.astype(jnp.float32) * grad_f32[:, None, :], axis=-1)
        dout = (
            (wgt[..., None] * grad_f32[:, None, :])
            .astype(jnp.bfloat16)
            .reshape(tok_rows * top_count, features)
        )
        dsend = to_buffer(dout, sources, 1)
        dreceived = as_rows(expert_exchange(dsend, 1))
        preact = lax.dynamic_index_in_dim(saved[4], fwd_index, 0, keepdims=False)

        def backward_live(operands):
            return expert_backward(operands[0], operands[1])

        dinbuf, dpre, dkept = lax.cond(live_step, backward_live, backward_skip, (dreceived, preact))
        dreturned = expert_exchange(as_pieces(dinbuf), 2)
        dexp = jnp.sum(from_buffer(dreturned, dest_rows).astype(jnp.float32), axis=1)
        dgate = (dwgt - jnp.sum(wgt * dwgt, axis=-1, keepdims=True)) / total
        dlogit = dgate * gatev * (1.0 - gatev)
        onehot = (route_rows[..., None] == expert_ids).astype(jnp.float32)
        dfull = jnp.sum(dlogit[..., None] * onehot, axis=1)
        drouter = jnp.dot(dfull, gate_cols.astype(jnp.float32).T, precision=lax.Precision.HIGHEST)
        dnorm = dexp + drouter
        grad_in = (
            grad_f32
            + rscale * dnorm
            - as_f32 * rscale**3 * jnp.mean(dnorm * as_f32, axis=-1, keepdims=True)
        ).astype(jnp.bfloat16)
        passed = from_behind(grad_in, "section", -1)
        return (passed, (dpre, dkept))

    start_grad = jnp.zeros((tok_rows, features), jnp.bfloat16)
    _, (dpre_all, dreceived_all) = lax.scan(backward_step, start_grad, jnp.arange(step_count))
    first_back = section_count - 1 - section_pos
    dpre_live = lax.dynamic_slice_in_dim(dpre_all, first_back, micro_count, axis=0)
    dreceived_live = lax.dynamic_slice_in_dim(dreceived_all, first_back, micro_count, axis=0)
    received_live = lax.dynamic_slice_in_dim(saved[3], section_pos, micro_count, axis=0)
    preact_live = lax.dynamic_slice_in_dim(saved[4], section_pos, micro_count, axis=0)
    hidden_live = jax.nn.gelu(preact_live).astype(jnp.bfloat16)
    rows_both = jnp.stack([received_live, dreceived_live])
    cols_both = jnp.stack([dpre_live, hidden_live])
    grads = jnp.einsum(
        "kbsecd,kbsech->kedh", rows_both, cols_both, preferred_element_type=jnp.float32
    )
    summed = ring_sum(grads.reshape(2, features, w_up.shape[2]), "dp")
    sum_up = summed[0].reshape(w_up.shape)
    sum_down = summed[1].T.reshape(w_down.shape)
    up_out = sum_up.astype(jnp.bfloat16)
    down_out = sum_down.astype(jnp.bfloat16)
    return (up_out[None], down_out[None])


def solution(mesh):
    in_specs = (
        P(None, ("dp", "expert"), None),
        P(None, ("dp", "expert"), None),
        P("section", "expert", None, None),
        P("section", "expert", None, None),
        P("section", None, None),
        P("section", None, ("dp", "expert"), None),
    )
    out_specs = (P("section", "expert", None, None), P("section", "expert", None, None))
    return jax.shard_map(local, mesh=mesh, in_specs=in_specs, out_specs=out_specs, check_vma=False)
```

```python
import functools

import jax
import jax.numpy as jnp
from jax import lax
from jax.experimental import pallas as pl
from jax.experimental.pallas import tpu as pltpu
from jax.sharding import PartitionSpec as P

MESH = pl.DeviceIdType.MESH

CAP = 17


epsilon = 1e-06


def from_behind(block, axis, distance):
    devices = range(lax.axis_size(axis))
    route = [(i - distance, i) for i in devices if i - distance in devices]
    return lax.ppermute(block, axis, route)


def exchange_kernel(n, x_ref, o_ref, copy_sem, send_sem, recv_sem):
    me = lax.axis_index("expert")
    barrier = pltpu.get_barrier_semaphore()
    for j in range(1, n):
        pl.semaphore_signal(
            barrier, inc=1, device_id={"expert": lax.rem(me + j, n)}, device_id_type=MESH
        )
    pl.semaphore_wait(barrier, n - 1)
    local = pltpu.make_async_copy(x_ref.at[me], o_ref.at[me], copy_sem)
    local.start()
    copies = []
    for j in range(1, n):
        peer = lax.rem(me + j, n)
        copy = pltpu.make_async_remote_copy(
            src_ref=x_ref.at[peer],
            dst_ref=o_ref.at[me],
            send_sem=send_sem.at[j],
            recv_sem=recv_sem.at[j],
            device_id={"expert": peer},
            device_id_type=MESH,
        )
        copy.start()
        copies.append(copy)
    local.wait()
    for copy in copies:
        copy.wait()


def expert_exchange(block, site):
    n = block.shape[0]
    nbytes = block.size * block.dtype.itemsize
    return pl.pallas_call(
        functools.partial(exchange_kernel, n),
        out_shape=jax.ShapeDtypeStruct(block.shape, block.dtype),
        in_specs=[pl.BlockSpec(memory_space=pl.ANY)],
        out_specs=pl.BlockSpec(memory_space=pl.ANY),
        scratch_shapes=[
            pltpu.SemaphoreType.DMA(()),
            pltpu.SemaphoreType.DMA((n,)),
            pltpu.SemaphoreType.DMA((n,)),
        ],
        compiler_params=pltpu.CompilerParams(collective_id=site, has_side_effects=True),
        cost_estimate=pl.CostEstimate(flops=0, bytes_accessed=2 * nbytes, transcendentals=0),
    )(block)


def ring_sum(flat, axis):
    count = lax.axis_size(axis)
    me = lax.axis_index(axis)
    halves = flat.reshape(2, count, -1, flat.shape[-1])
    results = []
    for half, way in ((0, 1), (1, -1)):
        own = halves[half]
        route = [(i, (i + way) % count) for i in range(count)]
        send = lax.dynamic_index_in_dim(own, me, 0, keepdims=False).astype(jnp.bfloat16)
        for step in range(count - 1):
            got = lax.ppermute(send, axis, route)
            chunk = lax.rem(me - way * (1 + step) + 2 * count, count)
            part = lax.dynamic_index_in_dim(own, chunk, 0, keepdims=False)
            send = (got.astype(jnp.float32) + part).astype(jnp.bfloat16)
        arrived = [send]
        for step in range(count - 1):
            send = lax.ppermute(send, axis, route)
            arrived.append(send)
        if way == 1:
            ordered = jnp.stack(arrived[1:][::-1] + [arrived[0]])
            first = lax.rem(count - 2 - me + 2 * count, count)
        else:
            ordered = jnp.stack(arrived)
            first = lax.rem(1 - me + 2 * count, count)
        doubled = jnp.concatenate([ordered, ordered])
        results.append(lax.dynamic_slice_in_dim(doubled, first, count, axis=0))
    return jnp.stack(results).reshape(flat.shape)


def normalize(section_in):
    as_f32 = section_in.astype(jnp.float32)
    rscale = lax.rsqrt(jnp.mean(as_f32 * as_f32, axis=-1, keepdims=True) + epsilon)
    return (as_f32, rscale, (as_f32 * rscale).astype(jnp.bfloat16))


def local(tokens, cotangent, up_proj, down_proj, gate_proj, routes):
    section_pos = lax.axis_index("section")
    section_count = lax.axis_size("section")
    expert_devs = lax.axis_size("expert")
    local_experts = up_proj.shape[1]
    experts_all = local_experts * expert_devs
    micro_count, tok_rows, features = tokens.shape
    top_count = routes.shape[3]
    capacity = CAP
    w_up = up_proj[0]
    w_down = down_proj[0]
    gate_cols = gate_proj[0]
    route_all = routes[0]
    step_count = micro_count + section_count - 1
    expert_ids = jnp.arange(experts_all, dtype=jnp.int32)

    def slot_rows(route_rows):
        flat_ids = route_rows.reshape(-1)
        onehot = (flat_ids[:, None] == expert_ids[None, :]).astype(jnp.int32)
        ranks = jnp.cumsum(onehot, axis=0) - onehot
        slots = jnp.sum(ranks * onehot, axis=1)
        return flat_ids * capacity + slots

    lanes = 128
    pieces = features // lanes

    def slot_sources(dest_rows):
        pair_ids = jnp.arange(dest_rows.shape[0], dtype=jnp.int32)
        slot_ids = jnp.arange(experts_all * capacity, dtype=jnp.int32)
        hits = dest_rows[:, None] == slot_ids[None, :]
        return jnp.max(jnp.where(hits, pair_ids[:, None], -1), axis=0)

    dest_all = jax.vmap(slot_rows)(route_all)
    source_all = jax.vmap(slot_sources)(dest_all)

    def to_buffer(row_values, sources, per_row):
        pieces_of = row_values.reshape(-1, pieces, lanes)
        picked = pieces_of[jnp.maximum(sources, 0) // per_row]
        filled = jnp.where((sources >= 0)[:, None, None], picked, jnp.zeros_like(picked))
        return filled.reshape(expert_devs, local_experts * capacity * pieces, lanes)

    def from_buffer(buffer, dest_rows):
        return buffer.reshape(experts_all * capacity, pieces, lanes)[dest_rows].reshape(
            tok_rows, top_count, features
        )

    def as_rows(buffer):
        return buffer.reshape(expert_devs, local_experts, capacity, features)

    def as_pieces(buffer):
        return buffer.reshape(expert_devs, local_experts * capacity * pieces, lanes)

    def gate_values(normed, route_rows):
        logits = jnp.dot(normed, gate_cols, preferred_element_type=jnp.float32)
        return jax.nn.sigmoid(jnp.take_along_axis(logits, route_rows, axis=1))

    def expert_forward(received):
        preact = jnp.einsum("secd,edh->sech", received, w_up, preferred_element_type=jnp.float32)
        hidden = jax.nn.gelu(preact).astype(jnp.bfloat16)
        outbuf = jnp.einsum(
            "sech,ehd->secd", hidden, w_down, preferred_element_type=jnp.float32
        ).astype(jnp.bfloat16)
        return (preact, outbuf)

    def expert_skip(received):
        preact = jnp.zeros(received.shape[:3] + (w_up.shape[2],), jnp.float32)
        return (preact, jnp.zeros_like(received))

    def forward_step(incoming, step_index):
        micro_raw = step_index - section_pos
        live_step = (micro_raw >= 0) & (micro_raw < micro_count)
        micro = jnp.clip(micro_raw, 0, micro_count - 1)
        first_in = lax.dynamic_index_in_dim(tokens, micro, 0, keepdims=False)
        section_in = jnp.where(section_pos == 0, first_in, incoming)
        route_rows = lax.dynamic_index_in_dim(route_all, micro, 0, keepdims=False)
        as_f32, rscale, normed = normalize(section_in)
        gatev = gate_values(normed, route_rows)
        wgt = gatev / jnp.sum(gatev, axis=-1, keepdims=True)
        dest_rows = lax.dynamic_index_in_dim(dest_all, micro, 0, keepdims=False)
        sources = lax.dynamic_index_in_dim(source_all, micro, 0, keepdims=False)
        received = as_rows(expert_exchange(to_buffer(normed, sources, top_count), 3))
        preact, outbuf = lax.cond(live_step, expert_forward, expert_skip, received)
        returned = expert_exchange(as_pieces(outbuf), 0)
        expout = from_buffer(returned, dest_rows)
        section_out = (
            as_f32 + jnp.sum(wgt[..., None] * expout.astype(jnp.float32), axis=1)
        ).astype(jnp.bfloat16)
        passed = from_behind(section_out, "section", 1)
        stored = (section_in, gatev, expout, received, preact)
        return (passed, stored)

    start_act = jnp.zeros((tok_rows, features), jnp.bfloat16)
    _, saved = lax.scan(forward_step, start_act, jnp.arange(step_count))

    def expert_backward(dreceived, preact):
        dhidden = jnp.einsum(
            "secd,ehd->sech", dreceived, w_down, preferred_element_type=jnp.float32
        )
        _, pullback = jax.vjp(jax.nn.gelu, preact)
        dpre = pullback(dhidden)[0].astype(jnp.bfloat16)
        dinbuf = jnp.einsum(
            "sech,edh->secd", dpre, w_up, preferred_element_type=jnp.float32
        ).astype(jnp.bfloat16)
        return (dinbuf, dpre, dreceived)

    def backward_skip(operands):
        dreceived, preact = operands
        return (
            jnp.zeros_like(dreceived),
            jnp.zeros(preact.shape, jnp.bfloat16),
            jnp.zeros_like(dreceived),
        )

    def backward_step(incoming, step_index):
        micro_raw = step_index - (section_count - 1 - section_pos)
        live_step = (micro_raw >= 0) & (micro_raw < micro_count)
        micro = jnp.clip(micro_raw, 0, micro_count - 1)
        fwd_index = micro + section_pos
        section_in = lax.dynamic_index_in_dim(saved[0], fwd_index, 0, keepdims=False)
        gatev = lax.dynamic_index_in_dim(saved[1], fwd_index, 0, keepdims=False)
        expout = lax.dynamic_index_in_dim(saved[2], fwd_index, 0, keepdims=False)
        last_in = lax.dynamic_index_in_dim(cotangent, micro, 0, keepdims=False)
        grad_out = jnp.where(section_pos == section_count - 1, last_in, incoming)
        route_rows = lax.dynamic_index_in_dim(route_all, micro, 0, keepdims=False)
        dest_rows = lax.dynamic_index_in_dim(dest_all, micro, 0, keepdims=False)
        sources = lax.dynamic_index_in_dim(source_all, micro, 0, keepdims=False)
        as_f32, rscale, _ = normalize(section_in)
        total = jnp.sum(gatev, axis=-1, keepdims=True)
        wgt = gatev / total
        grad_f32 = grad_out.astype(jnp.float32)
        dwgt = jnp.sum(expout.astype(jnp.float32) * grad_f32[:, None, :], axis=-1)
        dout = (
            (wgt[..., None] * grad_f32[:, None, :])
            .astype(jnp.bfloat16)
            .reshape(tok_rows * top_count, features)
        )
        dsend = to_buffer(dout, sources, 1)
        dreceived = as_rows(expert_exchange(dsend, 1))
        preact = lax.dynamic_index_in_dim(saved[4], fwd_index, 0, keepdims=False)

        def backward_live(operands):
            return expert_backward(operands[0], operands[1])

        dinbuf, dpre, dkept = lax.cond(live_step, backward_live, backward_skip, (dreceived, preact))
        dreturned = expert_exchange(as_pieces(dinbuf), 2)
        dexp = jnp.sum(from_buffer(dreturned, dest_rows).astype(jnp.float32), axis=1)
        dgate = (dwgt - jnp.sum(wgt * dwgt, axis=-1, keepdims=True)) / total
        dlogit = dgate * gatev * (1.0 - gatev)
        onehot = (route_rows[..., None] == expert_ids).astype(jnp.float32)
        dfull = jnp.sum(dlogit[..., None] * onehot, axis=1)
        drouter = jnp.dot(dfull, gate_cols.astype(jnp.float32).T, precision=lax.Precision.HIGHEST)
        dnorm = dexp + drouter
        grad_in = (
            grad_f32
            + rscale * dnorm
            - as_f32 * rscale**3 * jnp.mean(dnorm * as_f32, axis=-1, keepdims=True)
        ).astype(jnp.bfloat16)
        passed = from_behind(grad_in, "section", -1)
        return (passed, (dpre, dkept))

    start_grad = jnp.zeros((tok_rows, features), jnp.bfloat16)
    _, (dpre_all, dreceived_all) = lax.scan(backward_step, start_grad, jnp.arange(step_count))
    first_back = section_count - 1 - section_pos
    dpre_live = lax.dynamic_slice_in_dim(dpre_all, first_back, micro_count, axis=0)
    dreceived_live = lax.dynamic_slice_in_dim(dreceived_all, first_back, micro_count, axis=0)
    received_live = lax.dynamic_slice_in_dim(saved[3], section_pos, micro_count, axis=0)
    preact_live = lax.dynamic_slice_in_dim(saved[4], section_pos, micro_count, axis=0)
    hidden_live = jax.nn.gelu(preact_live).astype(jnp.bfloat16)
    rows_both = jnp.stack([received_live, dreceived_live])
    cols_both = jnp.stack([dpre_live, hidden_live])
    grads = jnp.einsum(
        "kbsecd,kbsech->kedh", rows_both, cols_both, preferred_element_type=jnp.float32
    )
    summed = ring_sum(grads.reshape(2, features, w_up.shape[2]), "dp")
    sum_up = summed[0].reshape(w_up.shape)
    sum_down = summed[1].T.reshape(w_down.shape)
    up_out = sum_up.astype(jnp.bfloat16)
    down_out = sum_down.astype(jnp.bfloat16)
    return (up_out[None], down_out[None])


def solution(mesh):
    in_specs = (
        P(None, ("dp", "expert"), None),
        P(None, ("dp", "expert"), None),
        P("section", "expert", None, None),
        P("section", "expert", None, None),
        P("section", None, None),
        P("section", None, ("dp", "expert"), None),
    )
    out_specs = (P("section", "expert", None, None), P("section", "expert", None, None))
    return jax.shard_map(local, mesh=mesh, in_specs=in_specs, out_specs=out_specs, check_vma=False)
```

```python
import functools

import jax
import jax.numpy as jnp
from jax import lax
from jax.experimental import pallas as pl
from jax.experimental.pallas import tpu as pltpu
from jax.sharding import PartitionSpec as P

MESH = pl.DeviceIdType.MESH

CAP = 17


epsilon = 1e-06


def from_behind(block, axis, distance):
    devices = range(lax.axis_size(axis))
    route = [(i - distance, i) for i in devices if i - distance in devices]
    return lax.ppermute(block, axis, route)


def exchange_kernel(n, x_ref, o_ref, copy_sem, send_sem, recv_sem):
    me = lax.axis_index("expert")
    barrier = pltpu.get_barrier_semaphore()
    for j in range(1, n):
        pl.semaphore_signal(
            barrier, inc=1, device_id={"expert": lax.rem(me + j, n)}, device_id_type=MESH
        )
    pl.semaphore_wait(barrier, n - 1)
    local = pltpu.make_async_copy(x_ref.at[me], o_ref.at[me], copy_sem)
    local.start()
    copies = []
    for j in range(1, n):
        peer = lax.rem(me + j, n)
        copy = pltpu.make_async_remote_copy(
            src_ref=x_ref.at[peer],
            dst_ref=o_ref.at[me],
            send_sem=send_sem.at[j],
            recv_sem=recv_sem.at[j],
            device_id={"expert": peer},
            device_id_type=MESH,
        )
        copy.start()
        copies.append(copy)
    local.wait()
    for copy in copies:
        copy.wait()


def expert_exchange(block, site):
    n = block.shape[0]
    nbytes = block.size * block.dtype.itemsize
    return pl.pallas_call(
        functools.partial(exchange_kernel, n),
        out_shape=jax.ShapeDtypeStruct(block.shape, block.dtype),
        in_specs=[pl.BlockSpec(memory_space=pl.ANY)],
        out_specs=pl.BlockSpec(memory_space=pl.ANY),
        scratch_shapes=[
            pltpu.SemaphoreType.DMA(()),
            pltpu.SemaphoreType.DMA((n,)),
            pltpu.SemaphoreType.DMA((n,)),
        ],
        compiler_params=pltpu.CompilerParams(collective_id=site, has_side_effects=True),
        cost_estimate=pl.CostEstimate(flops=0, bytes_accessed=2 * nbytes, transcendentals=0),
    )(block)


def ring_sum(flat, axis):
    count = lax.axis_size(axis)
    me = lax.axis_index(axis)
    halves = flat.reshape(2, count, -1, flat.shape[-1])
    results = []
    for half, way in ((0, 1), (1, -1)):
        own = halves[half]
        route = [(i, (i + way) % count) for i in range(count)]
        send = lax.dynamic_index_in_dim(own, me, 0, keepdims=False).astype(jnp.bfloat16)
        for step in range(count - 1):
            got = lax.ppermute(send, axis, route)
            chunk = lax.rem(me - way * (1 + step) + 2 * count, count)
            part = lax.dynamic_index_in_dim(own, chunk, 0, keepdims=False)
            send = (got.astype(jnp.float32) + part).astype(jnp.bfloat16)
        arrived = [send]
        for step in range(count - 1):
            send = lax.ppermute(send, axis, route)
            arrived.append(send)
        if way == 1:
            ordered = jnp.stack(arrived[1:][::-1] + [arrived[0]])
            first = lax.rem(count - 2 - me + 2 * count, count)
        else:
            ordered = jnp.stack(arrived)
            first = lax.rem(1 - me + 2 * count, count)
        doubled = jnp.concatenate([ordered, ordered])
        results.append(lax.dynamic_slice_in_dim(doubled, first, count, axis=0))
    return jnp.stack(results).reshape(flat.shape)


def normalize(section_in):
    as_f32 = section_in.astype(jnp.float32)
    rscale = lax.rsqrt(jnp.mean(as_f32 * as_f32, axis=-1, keepdims=True) + epsilon)
    return (as_f32, rscale, (as_f32 * rscale).astype(jnp.bfloat16))


def local(tokens, cotangent, up_proj, down_proj, gate_proj, routes):
    section_pos = lax.axis_index("section")
    section_count = lax.axis_size("section")
    expert_devs = lax.axis_size("expert")
    local_experts = up_proj.shape[1]
    experts_all = local_experts * expert_devs
    micro_count, tok_rows, features = tokens.shape
    top_count = routes.shape[3]
    capacity = CAP
    w_up = up_proj[0]
    w_down = down_proj[0]
    gate_cols = gate_proj[0]
    route_all = routes[0]
    step_count = micro_count + section_count - 1
    expert_ids = jnp.arange(experts_all, dtype=jnp.int32)

    def slot_rows(route_rows):
        flat_ids = route_rows.reshape(-1)
        onehot = (flat_ids[:, None] == expert_ids[None, :]).astype(jnp.int32)
        ranks = jnp.cumsum(onehot, axis=0) - onehot
        slots = jnp.sum(ranks * onehot, axis=1)
        return flat_ids * capacity + slots

    lanes = 128
    pieces = features // lanes

    def slot_sources(dest_rows):
        pair_ids = jnp.arange(dest_rows.shape[0], dtype=jnp.int32)
        slot_ids = jnp.arange(experts_all * capacity, dtype=jnp.int32)
        hits = dest_rows[:, None] == slot_ids[None, :]
        return jnp.max(jnp.where(hits, pair_ids[:, None], -1), axis=0)

    dest_all = jax.vmap(slot_rows)(route_all)
    source_all = jax.vmap(slot_sources)(dest_all)

    def to_buffer(row_values, sources, per_row):
        pieces_of = row_values.reshape(-1, pieces, lanes)
        picked = pieces_of[jnp.maximum(sources, 0) // per_row]
        filled = jnp.where((sources >= 0)[:, None, None], picked, jnp.zeros_like(picked))
        return filled.reshape(expert_devs, local_experts * capacity * pieces, lanes)

    def from_buffer(buffer, dest_rows):
        return buffer.reshape(experts_all * capacity, pieces, lanes)[dest_rows].reshape(
            tok_rows, top_count, features
        )

    def as_rows(buffer):
        return buffer.reshape(expert_devs, local_experts, capacity, features)

    def as_pieces(buffer):
        return buffer.reshape(expert_devs, local_experts * capacity * pieces, lanes)

    def gate_values(normed, route_rows):
        logits = jnp.dot(normed, gate_cols, preferred_element_type=jnp.float32)
        return jax.nn.sigmoid(jnp.take_along_axis(logits, route_rows, axis=1))

    def expert_forward(received):
        preact = jnp.einsum("secd,edh->sech", received, w_up, preferred_element_type=jnp.float32)
        hidden = jax.nn.gelu(preact).astype(jnp.bfloat16)
        outbuf = jnp.einsum(
            "sech,ehd->secd", hidden, w_down, preferred_element_type=jnp.float32
        ).astype(jnp.bfloat16)
        return (preact, outbuf)

    def expert_skip(received):
        preact = jnp.zeros(received.shape[:3] + (w_up.shape[2],), jnp.float32)
        return (preact, jnp.zeros_like(received))

    def forward_step(incoming, step_index):
        micro_raw = step_index - section_pos
        live_step = (micro_raw >= 0) & (micro_raw < micro_count)
        micro = jnp.clip(micro_raw, 0, micro_count - 1)
        first_in = lax.dynamic_index_in_dim(tokens, micro, 0, keepdims=False)
        section_in = jnp.where(section_pos == 0, first_in, incoming)
        route_rows = lax.dynamic_index_in_dim(route_all, micro, 0, keepdims=False)
        as_f32, rscale, normed = normalize(section_in)
        gatev = gate_values(normed, route_rows)
        wgt = gatev / jnp.sum(gatev, axis=-1, keepdims=True)
        dest_rows = lax.dynamic_index_in_dim(dest_all, micro, 0, keepdims=False)
        sources = lax.dynamic_index_in_dim(source_all, micro, 0, keepdims=False)
        received = as_rows(expert_exchange(to_buffer(normed, sources, top_count), 3))
        preact, outbuf = lax.cond(live_step, expert_forward, expert_skip, received)
        returned = expert_exchange(as_pieces(outbuf), 0)
        expout = from_buffer(returned, dest_rows)
        section_out = (
            as_f32 + jnp.sum(wgt[..., None] * expout.astype(jnp.float32), axis=1)
        ).astype(jnp.bfloat16)
        passed = from_behind(section_out, "section", 1)
        stored = (section_in, gatev, expout, received, preact)
        return (passed, stored)

    start_act = jnp.zeros((tok_rows, features), jnp.bfloat16)
    _, saved = lax.scan(forward_step, start_act, jnp.arange(step_count))

    def expert_backward(dreceived, preact):
        dhidden = jnp.einsum(
            "secd,ehd->sech", dreceived, w_down, preferred_element_type=jnp.float32
        )
        _, pullback = jax.vjp(jax.nn.gelu, preact)
        dpre = pullback(dhidden)[0].astype(jnp.bfloat16)
        dinbuf = jnp.einsum(
            "sech,edh->secd", dpre, w_up, preferred_element_type=jnp.float32
        ).astype(jnp.bfloat16)
        return (dinbuf, dpre)

    def backward_skip(operands):
        dreceived, preact = operands
        return (jnp.zeros_like(dreceived), jnp.zeros(preact.shape, jnp.bfloat16))

    def backward_step(incoming, step_index):
        micro_raw = step_index - (section_count - 1 - section_pos)
        live_step = (micro_raw >= 0) & (micro_raw < micro_count)
        micro = jnp.clip(micro_raw, 0, micro_count - 1)
        fwd_index = micro + section_pos
        section_in = lax.dynamic_index_in_dim(saved[0], fwd_index, 0, keepdims=False)
        gatev = lax.dynamic_index_in_dim(saved[1], fwd_index, 0, keepdims=False)
        expout = lax.dynamic_index_in_dim(saved[2], fwd_index, 0, keepdims=False)
        last_in = lax.dynamic_index_in_dim(cotangent, micro, 0, keepdims=False)
        grad_out = jnp.where(section_pos == section_count - 1, last_in, incoming)
        route_rows = lax.dynamic_index_in_dim(route_all, micro, 0, keepdims=False)
        dest_rows = lax.dynamic_index_in_dim(dest_all, micro, 0, keepdims=False)
        sources = lax.dynamic_index_in_dim(source_all, micro, 0, keepdims=False)
        as_f32, rscale, _ = normalize(section_in)
        total = jnp.sum(gatev, axis=-1, keepdims=True)
        wgt = gatev / total
        grad_f32 = grad_out.astype(jnp.float32)
        dwgt = jnp.sum(expout.astype(jnp.float32) * grad_f32[:, None, :], axis=-1)
        dout = (
            (wgt[..., None] * grad_f32[:, None, :])
            .astype(jnp.bfloat16)
            .reshape(tok_rows * top_count, features)
        )
        dsend = to_buffer(dout, sources, 1)
        dreceived = as_rows(expert_exchange(dsend, 1))
        preact = lax.dynamic_index_in_dim(saved[4], fwd_index, 0, keepdims=False)

        def backward_live(operands):
            return expert_backward(operands[0], operands[1])

        dinbuf, dpre = lax.cond(live_step, backward_live, backward_skip, (dreceived, preact))
        dreturned = expert_exchange(as_pieces(dinbuf), 2)
        dexp = jnp.sum(from_buffer(dreturned, dest_rows).astype(jnp.float32), axis=1)
        dgate = (dwgt - jnp.sum(wgt * dwgt, axis=-1, keepdims=True)) / total
        dlogit = dgate * gatev * (1.0 - gatev)
        onehot = (route_rows[..., None] == expert_ids).astype(jnp.float32)
        dfull = jnp.sum(dlogit[..., None] * onehot, axis=1)
        drouter = jnp.dot(dfull, gate_cols.astype(jnp.float32).T, precision=lax.Precision.HIGHEST)
        dnorm = dexp + drouter
        grad_in = (
            grad_f32
            + rscale * dnorm
            - as_f32 * rscale**3 * jnp.mean(dnorm * as_f32, axis=-1, keepdims=True)
        ).astype(jnp.bfloat16)
        passed = from_behind(grad_in, "section", -1)
        return (passed, (dpre, dreceived))

    start_grad = jnp.zeros((tok_rows, features), jnp.bfloat16)
    _, (dpre_all, dreceived_all) = lax.scan(backward_step, start_grad, jnp.arange(step_count))
    first_back = section_count - 1 - section_pos
    dpre_live = lax.dynamic_slice_in_dim(dpre_all, first_back, micro_count, axis=0)
    dreceived_live = lax.dynamic_slice_in_dim(dreceived_all, first_back, micro_count, axis=0)
    received_live = lax.dynamic_slice_in_dim(saved[3], section_pos, micro_count, axis=0)
    preact_live = lax.dynamic_slice_in_dim(saved[4], section_pos, micro_count, axis=0)
    hidden_live = jax.nn.gelu(preact_live).astype(jnp.bfloat16)
    rows_both = jnp.stack([received_live, dreceived_live])
    cols_both = jnp.stack([dpre_live, hidden_live])
    grads = jnp.einsum(
        "kbsecd,kbsech->kedh", rows_both, cols_both, preferred_element_type=jnp.float32
    )
    summed = ring_sum(grads.reshape(2, features, w_up.shape[2]), "dp")
    sum_up = summed[0].reshape(w_up.shape)
    sum_down = summed[1].T.reshape(w_down.shape)
    up_out = sum_up.astype(jnp.bfloat16)
    down_out = sum_down.astype(jnp.bfloat16)
    return (up_out[None], down_out[None])


def solution(mesh):
    in_specs = (
        P(None, ("dp", "expert"), None),
        P(None, ("dp", "expert"), None),
        P("section", "expert", None, None),
        P("section", "expert", None, None),
        P("section", None, None),
        P("section", None, ("dp", "expert"), None),
    )
    out_specs = (P("section", "expert", None, None), P("section", "expert", None, None))
    return jax.shard_map(local, mesh=mesh, in_specs=in_specs, out_specs=out_specs, check_vma=False)
```
